256 devices in a mesh: tx: 8 (over z), ty: 2 (over y_lo), vel: 16 (over x, y_hi, core).
Axes of the slice: x: 4, y: 4 (y_hi: 2, y_lo: 2; y = y_hi * 2 + y_lo), z: 8, core: 2. Of those that a mesh axis runs over, the one named last changes fastest.
Arguments:
- initial: float32 [64, 16, 16, 12288], P('tx', 'ty', None, 'vel'), may hold values from -2 to 3.5
- velocity: float32 [3, 12288], P(None, 'vel'), may hold values from -3 to 3, as said below
- weights: float32 [12288], P('vel'), may hold values from 0.5 to 2
- wall: int32 [64, 16, 16], P('tx', 'ty'), may hold values 0 or 1
- wall_temp: float32 [64, 16, 16], P('tx', 'ty'), may hold values from -1 to 1
- mass_target: float32 [], replicated, may hold values from 0.5 to 1.5
Outputs:
- distribution: float32 [64, 16, 16, 12288], P('tx', 'ty', None, 'vel')
- macro_fields: float32 [5, 64, 16, 16], P(None, 'tx', 'ty')
The draws below stay inside these ranges and needn't reach their ends.
Inputs may be any that keep to these rules, and one draw needn't show every extreme that they name: `velocity`: within each aligned block of 768 velocities the first quarter has positive x and y components, the second positive x and negative y, the third negative x and positive y, the fourth negative x and y; x and y components are 0.05 or more in magnitude.
All inputs are finite; a program needn't handle non-finite values. No bound on the sum of `wall` on one device may be relied on, other than what follows from the above.
Results may differ from the reference program's by a relative error of at most 0.0003.
Values sent between devices are 32-bit elements; how exact they have to be, the bound alone decides.
A program may use at most 128 MiB of HBM per device.

```python
import math
import jax
import jax.numpy as jnp
from jax import lax

NZ = 16
V_DEV = 768
ITERS = 3
MACRO_STEPS = 4
NX = 64
NY = 16
V = 12288
N_VEL = 16


def draw_initial(key, part):
    rough_key = jax.random.fold_in(jax.random.fold_in(key, 11), 0)
    position = (jnp.arange(NX, dtype=jnp.float32) / NX)[:, None, None, None]
    rough_part = jnp.clip(jax.random.normal(rough_key, (NX, NY, NZ, V), jnp.float32), -4.0, 4.0)
    return 0.5 * rough_part + (0.3 + 0.6 * position)


def draw_velocity(key, part):
    size_key, lateral_key = jax.random.split(jax.random.fold_in(key, 23))
    slot_index = jnp.arange(V) % V_DEV
    quarter_index = slot_index // (V_DEV // 4)
    sign_x = jnp.where(quarter_index < 2, 1.0, -1.0)
    sign_y = jnp.where(quarter_index % 2 == 0, 1.0, -1.0)
    sizes = jnp.minimum(jnp.abs(jax.random.normal(size_key, (2, V), jnp.float32)), 2.95)
    lateral = jnp.clip(jax.random.normal(lateral_key, (V,), jnp.float32), -3.0, 3.0)
    return jnp.stack([sign_x * (0.05 + sizes[0]), sign_y * (0.05 + sizes[1]), lateral])


def touch_ends(values, own_key, low, high):
    shape = values.shape
    spot = [jax.random.randint(jax.random.fold_in(own_key, axis), (), 0, shape[axis]) for axis in range(len(shape))]
    values = values.at[tuple(spot)].set(low)
    longest = shape.index(max(shape))
    spot[longest] = (spot[longest] + 1) % shape[longest]
    return values.at[tuple(spot)].set(high)


def steps_of(key, extent, shards, smallest, high):
    def one(axis_at, shards_of):
        draws = jax.random.uniform(jax.random.fold_in(jax.random.fold_in(key, 6), axis_at), (shards_of,), jnp.float32, smallest / len(shards), high / len(shards))
        return jnp.repeat(jnp.exp(draws), extent[axis_at] // shards_of).reshape((-1,) + (1,) * (len(extent) - axis_at - 1))

    level = one(*shards[0])
    for cut in shards[1:]:
        level = level * one(*cut)
    return level


def setup_inputs(seed: int = 0) -> dict:
    streams_of = jax.random.split(jax.random.key(seed), 7)
    initial = draw_initial(jax.random.fold_in(streams_of[6], 71), 0)
    velocity = draw_velocity(jax.random.fold_in(streams_of[6], 71), 0)
    weights = jnp.clip(jnp.exp(math.log(2.0) - 1.3862944 * jax.random.uniform(streams_of[2], (V,), jnp.float32) ** steps_of(streams_of[2], (V,), ((0, 16),), -0.2, 0.2)), 0.5, 2.0)
    wall = touch_ends((jax.random.randint(streams_of[3], (NX, NY, NZ), 0, 8) < 1).astype(jnp.int32), jax.random.fold_in(streams_of[3], 1), 0, 1)
    wall_temp = jnp.clip(jax.random.uniform(streams_of[4], (NX, NY, NZ), jnp.float32, -1.0, 1.0) * steps_of(streams_of[4], (NX, NY, NZ), ((0, 8), (1, 2)), -0.4, 0.0), -1.0, 1.0)
    mass_target = jnp.clip(jax.random.uniform(streams_of[5], (), jnp.float32, 0.5, 1.5), 0.5, 1.5)
    return dict(initial=initial, velocity=velocity, weights=weights, wall=wall, wall_temp=wall_temp, mass_target=mass_target)


step_time = 0.1
collision = 1.0
macro_time = 0.1
viscosity = 1.0
conduction = 1.0
highest = lax.Precision.HIGHEST


def basis(velocity):
    speed_sq = velocity[0] * velocity[0] + velocity[1] * velocity[1] + velocity[2] * velocity[2]
    return jnp.stack([jnp.ones_like(speed_sq), 2.0 * velocity[0], 2.0 * velocity[1], 2.0 * velocity[2], speed_sq - 1.5])


def projector(velocity, weights, total_count):
    vel_x, vel_y, vel_z = velocity[0], velocity[1], velocity[2]
    speed_sq = vel_x * vel_x + vel_y * vel_y + vel_z * vel_z
    moment_rows = jnp.stack([jnp.ones_like(speed_sq), vel_x, vel_y, vel_z, (2.0 / 3.0) * speed_sq - 1.0,
                             2.0 * (vel_x * vel_x - speed_sq / 3.0), 2.0 * (vel_y * vel_y - speed_sq / 3.0),
                             2.0 * (vel_z * vel_z - speed_sq / 3.0), 2.0 * vel_x * vel_y, 2.0 * vel_x * vel_z,
                             2.0 * vel_y * vel_z, vel_x * (speed_sq - 2.5), vel_y * (speed_sq - 2.5),
                             vel_z * (speed_sq - 2.5)])
    return moment_rows * (weights / total_count)[None, :]


def differences(shifted):
    grads = [(shifted(direction, 1) - shifted(direction, -1)) * 0.5 for direction in (1, 2, 3)]
    middle = shifted(1, 0)
    laplace = (shifted(1, 1) + shifted(1, -1) - 2.0 * middle) + (shifted(2, 1) + shifted(2, -1) - 2.0 * middle)
    laplace = laplace + (shifted(3, 1) + shifted(3, -1) - 2.0 * middle)
    return grads, laplace, middle


def macro_sources(shifted):
    grads, laplace, middle = differences(shifted)
    grad_x, grad_y, grad_z = grads
    sig_x = grad_x[0] + grad_y[3] + grad_z[4]
    sig_y = grad_x[3] + grad_y[1] + grad_z[5]
    sig_z = grad_x[4] + grad_y[5] + grad_z[2]
    heat_flow = grad_x[6] + grad_y[7] + grad_z[8]
    return jnp.stack([-0.5 * (sig_x + viscosity * laplace[9]), -0.5 * (sig_y + viscosity * laplace[10]),
                      -0.5 * (sig_z + viscosity * laplace[11]), -(2.0 / 3.0) * (heat_flow + conduction * laplace[12])])


def macro_step(shifted, sources):
    grads, laplace, middle = differences(shifted)
    grad_x, grad_y, grad_z = grads
    div_u = grad_x[1] + grad_y[2] + grad_z[3]
    change_rates = [-div_u]
    for component in range(3):
        along = grads[component]
        change_rates.append(-0.5 * (along[0] + along[4]) + 0.5 * viscosity * laplace[1 + component] + sources[component])
    change_rates.append(-(2.0 / 3.0) * div_u + (2.0 / 3.0) * conduction * laplace[4] + sources[3])
    return middle + macro_time * jnp.stack(change_rates)


def kinetic_update(corrected, equilibrium, before_x, after_x, before_y, after_y, velocity):
    plus_part = jnp.maximum(velocity, 0.0)
    minus_part = jnp.minimum(velocity, 0.0)
    before_z = jnp.roll(corrected, 1, 2)
    after_z = jnp.roll(corrected, -1, 2)
    transport = plus_part[0] * (corrected - before_x) + minus_part[0] * (after_x - corrected)
    transport = transport + (plus_part[1] * (corrected - before_y) + minus_part[1] * (after_y - corrected))
    transport = transport + (plus_part[2] * (corrected - before_z) + minus_part[2] * (after_z - corrected))
    return corrected - step_time * transport + (step_time * collision) * (equilibrium - corrected)


def rolled(stack):
    def shifted(direction, offset):
        return jnp.roll(stack, -offset, direction)
    return shifted


def reference(initial, velocity, weights, wall, wall_temp, mass_target):
    block_count = N_VEL
    block_width = V // N_VEL
    state_f = jnp.moveaxis(initial.reshape(NX, NY, NZ, block_count, block_width), 3, 0)
    vel_blocks = jnp.moveaxis(velocity.reshape(3, block_count, block_width), 1, 0)
    weight_blocks = weights.reshape(block_count, block_width)
    is_wall = (wall == 1)[..., None]
    cell_count = float(NX * NY * NZ)
    macro_state = None
    for iteration in range(ITERS):
        def block_moments(pieces):
            dist_slab, vel_slab, weight_slab = pieces
            return jnp.einsum("kv,xyzv->kxyz", projector(vel_slab, weight_slab, float(V)), dist_slab,
                              precision=highest)

        moments = jnp.sum(lax.map(block_moments, (state_f, vel_blocks, weight_blocks)), axis=0)
        kinetic_state = moments[0:5]
        fields = jnp.concatenate([moments[5:14], moments[1:5]])
        sources = macro_sources(rolled(fields))
        macro_state = kinetic_state
        for sweep in range(MACRO_STEPS):
            macro_state = macro_step(rolled(macro_state), sources)
        density_mean = jnp.sum(macro_state[0]) / cell_count
        macro_state = jnp.concatenate([((macro_state[0] - density_mean) + mass_target)[None], macro_state[1:]])
        change = macro_state - kinetic_state
        current_state = macro_state

        def block_kinetic(pieces):
            dist_slab, vel_slab = pieces
            rows = basis(vel_slab)
            corrected = dist_slab + jnp.einsum("kxyz,kv->xyzv", change, rows, precision=highest)
            equilibrium = jnp.einsum("kxyz,kv->xyzv", current_state, rows, precision=highest)
            updated = kinetic_update(corrected, equilibrium, jnp.roll(corrected, 1, 0), jnp.roll(corrected, -1, 0),
                                     jnp.roll(corrected, 1, 1), jnp.roll(corrected, -1, 1), vel_slab)
            return jnp.where(is_wall, wall_temp[..., None] * rows[4], updated)

        state_f = lax.map(block_kinetic, (state_f, vel_blocks))
    distribution = jnp.moveaxis(state_f, 0, 3).reshape(NX, NY, NZ, V)
    return distribution, macro_state
```

```python
import functools

import jax
import jax.numpy as jnp
from jax import lax
from jax.experimental import pallas as pl
from jax.experimental.pallas import tpu as pltpu
from jax.sharding import PartitionSpec as P

ITERS = 3
MACRO_STEPS = 4
NCOMP = 14
MASS = 14
STEP = 0.1
f32 = jnp.float32
bf16 = jnp.bfloat16
MESH = pl.DeviceIdType.MESH
NX, NY, NZ, NV = 8, 8, 16, 768
CELLS = NY * NZ
ROWS = 48
COEF = 40
NEIGHBOURS = [(0, -1), (0, 1), (1, -1), (1, 0), (1, 1)]


def nt(a, b, precision=None):
    return lax.dot_general(a, b, (((1,), (1,)), ((), ())), precision=precision, preferred_element_type=f32)


def tn(a, b):
    return lax.dot_general(a, b, (((0,), (0,)), ((), ())), preferred_element_type=f32)


def rounded(value):
    return value.astype(bf16).astype(f32)


def lanes_of(value):
    return lax.broadcasted_iota(jnp.int32, value.shape, 1)


def other_half(value):
    parts = value.reshape(-1, 2, ROWS // 2, CELLS)
    return jnp.concatenate([parts[:, 1:2], parts[:, 0:1]], axis=1).reshape(value.shape)


def x_next(v):
    return pltpu.roll(v, v.shape[0] - 1, 0)


def x_last(v):
    return pltpu.roll(v, 1, 0)


def y_next(v):
    r = pltpu.roll(v, CELLS - NZ, 1)
    return jnp.where(lanes_of(v) < CELLS - NZ, r, other_half(r))


def y_last(v):
    r = pltpu.roll(v, NZ, 1)
    return jnp.where(lanes_of(v) >= NZ, r, other_half(r))


def z_next(v):
    z = lax.rem(lanes_of(v), NZ)
    return jnp.where(z == NZ - 1, pltpu.roll(v, NZ - 1, 1), pltpu.roll(v, CELLS - 1, 1))


def z_last(v):
    z = lax.rem(lanes_of(v), NZ)
    return jnp.where(z == 0, pltpu.roll(v, CELLS - NZ + 1, 1), pltpu.roll(v, 1, 1))


def field(v, k):
    return v[k * ROWS : (k + 1) * ROWS]


def kernel(
    sizes,
    init_ref, vel_ref, weight_ref, wall_ref, wall_temp_ref, target_ref,
    dist_ref, macro_ref,
    h, stream, edge_y, part, stream_part, rs, near, gathered, tile_mass, mass,
    coef, coef3, rows_f, rows3, proj_f, proj2, mixed3, factors, open_cells, wall_rows, state, source,
    load_sem, rs_send, rs_recv, near_send, near_recv, all_send, all_recv,
    tile_send, tile_recv, mass_send, mass_recv, edge_send, edge_recv,
):
    n_tx, n_ty, n_vel = sizes
    tx, ty, me = lax.axis_index("tx"), lax.axis_index("ty"), lax.axis_index("vel")

    def device(dx, dy, vel):
        return {"tx": lax.rem(tx + (dx + n_tx), n_tx), "ty": lax.rem(ty + dy, n_ty), "vel": vel}

    def group(step):
        return lax.rem(me + step, n_vel)

    far_tiles = [(a, b) for b in range(n_ty) for a in range(n_tx) if (a, b) != (0, 0)]
    near_tiles = [(dx % n_tx, dy) for dy, dx in NEIGHBOURS]
    only_far = [t for t in far_tiles if t not in near_tiles]

    load = pltpu.make_async_copy(init_ref, h.at[0, 0:NX, 0:NY], load_sem)
    load.start()

    barrier = pltpu.get_barrier_semaphore()
    for step in range(1, n_vel):
        pl.semaphore_signal(barrier, inc=1, device_id=device(0, 0, group(step)), device_id_type=MESH)
    for a, b in near_tiles:
        pl.semaphore_signal(barrier, inc=1, device_id=device(a, b, me), device_id_type=MESH)

    @pl.when(me == MASS)
    def _():
        for a, b in only_far:
            pl.semaphore_signal(barrier, inc=1, device_id=device(a, b, me), device_id_type=MESH)

    vx, vy, vz = vel_ref[0:1, :], vel_ref[1:2, :], vel_ref[2:3, :]
    speed_sq = vx * vx + vy * vy + vz * vz
    ones = jnp.ones_like(vx)
    basis = [ones, 2.0 * vx, 2.0 * vy, 2.0 * vz, speed_sq - 1.5]
    sides = []
    for v in (vx, vy, vz):
        sides += [STEP * jnp.maximum(v, 0.0), -STEP * jnp.minimum(v, 0.0)]
    rows = basis + [side * b for side in sides for b in basis] + [basis[4]]
    for copy in range(3):
        for at, row in enumerate(rows):
            rows_f[copy * COEF + at : copy * COEF + at + 1, :] = row
        rows_f[copy * COEF + len(rows) : (copy + 1) * COEF, :] = jnp.zeros((COEF - len(rows), NV), f32)
    rows_f[3 * COEF :, :] = jnp.zeros((128 - 3 * COEF, NV), f32)
    scale = weight_ref[0:1, :] / float(NV * n_vel)
    moments = [ones, vx, vy, vz, (2.0 / 3.0) * speed_sq - 1.0,
               2.0 * (vx * vx - speed_sq / 3.0), 2.0 * (vy * vy - speed_sq / 3.0), 2.0 * (vz * vz - speed_sq / 3.0),
               2.0 * vx * vy, 2.0 * vx * vz, 2.0 * vy * vz,
               vx * (speed_sq - 2.5), vy * (speed_sq - 2.5), vz * (speed_sq - 2.5), ones]
    for at, row in enumerate(moments):
        proj_f[at : at + 1, :] = row * scale
    proj_f[15:16, :] = jnp.zeros((1, NV), f32)
    bx, by, bz = (STEP * jnp.abs(v) for v in (vx, vy, vz))
    for at, row in enumerate((0.9 - bx - by - bz, bx, by, bz, vz)):
        factors[at : at + 1, :] = row
    every = rows_f[...]
    high = rounded(every)
    rows3[...] = jnp.where(lax.broadcasted_iota(jnp.int32, every.shape, 0) < 2 * COEF, high, every - high).astype(bf16)
    proj = proj_f[...]
    proj2[...] = jnp.concatenate([rounded(proj), proj - rounded(proj)], axis=0).astype(bf16)
    mixed = nt(proj, every, lax.Precision.HIGHEST)
    mixed_high = rounded(mixed)
    mixed3[...] = jnp.where(lanes_of(mixed) < 2 * COEF, mixed_high, mixed - mixed_high).astype(bf16)

    solid = jnp.zeros((NX, CELLS), f32)
    heat = jnp.zeros((NX, CELLS), f32)
    for y in range(NY):
        spread = (lax.broadcasted_iota(jnp.int32, (NZ, CELLS), 1)
                  == lax.broadcasted_iota(jnp.int32, (NZ, CELLS), 0) + y * NZ).astype(f32)
        is_wall = (wall_ref[:, y, :] == 1).astype(f32)
        solid = solid + lax.dot_general(is_wall, spread, (((1,), (0,)), ((), ())), precision=lax.Precision.HIGHEST,
                                        preferred_element_type=f32)
        heat = heat + lax.dot_general(is_wall * wall_temp_ref[:, y, :], spread, (((1,), (0,)), ((), ())),
                                      precision=lax.Precision.HIGHEST, preferred_element_type=f32)
    fluid = 1.0 - solid
    wall_rows[0] = fluid
    for x in range(NX):
        open_cells[x] = jnp.broadcast_to(fluid[x : x + 1], (CELLS, CELLS)).T
    coef[35 * NX : 36 * NX, :] = heat
    coef[36 * NX :, :] = jnp.zeros((4 * NX, CELLS), f32)

    def projected(value):
        top = value.astype(bf16)
        low = (value - top.astype(f32)).astype(bf16)
        both = nt(proj2[...], top)
        return both[0:16] + both[16:32] + nt(proj2[0:16, :], low)

    def plane(it, x):
        return h[it, x, 0:NY].reshape(CELLS, NV)

    def pack_edges(it):
        def body(x, _):
            top, bottom = h[it, x, NY - 1], h[it, x, 0]
            for t in range(6):
                cut = slice(t * 128, (t + 1) * 128)
                if t in (0, 3):
                    piece = top[:, cut]
                elif t in (2, 5):
                    piece = bottom[:, cut]
                else:
                    piece = jnp.where(lanes_of(top[:, cut]) < 64, top[:, cut], bottom[:, cut])
                edge_y[it, x, :, cut] = piece
            return 0

        lax.fori_loop(0, NX, body, 0)

    def edge_copies(it):
        half = NV // 2
        return [
            pltpu.make_async_remote_copy(
                src_ref=edge_y.at[it], dst_ref=h.at[it, 0:NX, NY],
                send_sem=edge_send.at[it, 0], recv_sem=edge_recv.at[it, 0],
                device_id=device(0, 1, me), device_id_type=MESH),
            pltpu.make_async_remote_copy(
                src_ref=h.at[it, NX - 1, 0:NY, :, 0:half], dst_ref=h.at[it, NX, 0:NY, :, 0:half],
                send_sem=edge_send.at[it, 1], recv_sem=edge_recv.at[it, 1],
                device_id=device(1, 0, me), device_id_type=MESH),
            pltpu.make_async_remote_copy(
                src_ref=h.at[it, 0, 0:NY, :, half:NV], dst_ref=h.at[it, NX, 0:NY, :, half:NV],
                send_sem=edge_send.at[it, 2], recv_sem=edge_recv.at[it, 2],
                device_id=device(-1, 0, me), device_id_type=MESH),
        ]

    def stream_cell(it, x, y):
        half = NV // 2
        x_down, x_up = lax.rem(x + NX, NX + 1), x + 1
        y_down, y_up = (y + NY) % (NY + 1), y + 1
        for t in range(6):
            cut = slice(t * 128, (t + 1) * 128)
            own = h[it, x, y, :, cut]
            from_x = h[it, x_down if t < 3 else x_up, y, :, cut]
            if t in (0, 3):
                from_y = h[it, x, y_down, :, cut]
            elif t in (2, 5):
                from_y = h[it, x, y_up, :, cut]
            else:
                from_y = jnp.where(lanes_of(own) < 64, h[it, x, y_down, :, cut], h[it, x, y_up, :, cut])
            up = jnp.broadcast_to(factors[4:5, cut], own.shape) > 0.0
            from_z = jnp.where(up, pltpu.roll(own, 1, 0), pltpu.roll(own, NZ - 1, 0))
            value = (factors[0:1, cut] * own + factors[1:2, cut] * from_x
                     + factors[2:3, cut] * from_y + factors[3:4, cut] * from_z)
            stream[x, y, :, cut] = value * open_cells[x, y * NZ : (y + 1) * NZ, :]

    def stream_inside(it):
        def body(x, _):
            for y in range(1, NY - 1):
                stream_cell(it, x, y)
            return 0

        lax.fori_loop(1, NX - 1, body, 0)

    def stream_edges(it):
        def body(x, _):
            stream_cell(it, x, 0)
            stream_cell(it, x, NY - 1)
            return 0

        lax.fori_loop(0, NX, body, 0)

        def ends(side, _):
            for y in range(1, NY - 1):
                stream_cell(it, side * (NX - 1), y)
            return 0

        lax.fori_loop(0, 2, ends, 0)

    def rs_copy(it, step):
        target = group(step)
        return target, pltpu.make_async_remote_copy(
            src_ref=part.at[pl.ds(pl.multiple_of(target * NX, NX), NX)], dst_ref=rs.at[it, step - 1],
            send_sem=rs_send.at[it, step - 1], recv_sem=rs_recv.at[it, step - 1],
            device_id=device(0, 0, target), device_id_type=MESH)

    def near_copies(it):
        return [
            pltpu.make_async_remote_copy(
                src_ref=near.at[it, 1], dst_ref=near.at[it, dy * 3 + 1 - dx],
                send_sem=near_send.at[it, at], recv_sem=near_recv.at[it, dy * 3 + 1 - dx],
                device_id=device(dx, dy, me), device_id_type=MESH)
            for at, (dy, dx) in enumerate(NEIGHBOURS)
        ]

    def all_copy(it, step):
        return pltpu.make_async_remote_copy(
            src_ref=near.at[it], dst_ref=gathered.at[it, me],
            send_sem=all_send.at[it, step - 1], recv_sem=all_recv.at[it, me],
            device_id=device(0, 0, group(step)), device_id_type=MESH)

    def tile_copies(it):
        return [
            pltpu.make_async_remote_copy(
                src_ref=near.at[it, 1], dst_ref=tile_mass.at[it, at],
                send_sem=tile_send.at[it, at], recv_sem=tile_recv.at[it, at],
                device_id=device(a, b, me), device_id_type=MESH)
            for at, (a, b) in enumerate(far_tiles)
        ]

    def mass_copy(it, step):
        return pltpu.make_async_remote_copy(
            src_ref=mass.at[it], dst_ref=mass.at[it],
            send_sem=mass_send.at[it, step - 1], recv_sem=mass_recv.at[it],
            device_id=device(0, 0, group(step)), device_id_type=MESH)

    def macro_solve(it):
        def g(c):
            return gathered[it, c].reshape(ROWS, CELLS)

        def many(*cs):
            return jnp.concatenate([g(c) for c in cs], axis=0)

        flow = many(1, 2, 3, 4)
        along = (many(5, 8, 9, 11), many(8, 6, 10, 12), many(9, 10, 7, 13))
        shifts = ((x_next, x_last), (y_next, y_last), (z_next, z_last))
        total = -6.0 * flow
        for (after, before), a in zip(shifts, along):
            total = total + (after(flow + 0.5 * a) + before(flow - 0.5 * a))
        source[0 : 3 * ROWS] = -0.5 * total[0 : 3 * ROWS]
        source[3 * ROWS :] = -(2.0 / 3.0) * total[3 * ROWS :]
        state[...] = many(0, 1, 2, 3, 4)

        def sweep(_, carry):
            rho, flow = state[0:ROWS], state[ROWS : 5 * ROWS]
            stack = jnp.concatenate([rho + field(flow, 3), flow], axis=0)
            laplace = -6.0 * flow
            grads, divergence = [], None
            for d, (after, before) in enumerate(shifts):
                up, down = after(stack), before(stack)
                laplace = laplace + (up[ROWS:] + down[ROWS:])
                grads.append(0.5 * (field(up, 0) - field(down, 0)))
                part_div = 0.5 * (field(up, 1 + d) - field(down, 1 + d))
                divergence = part_div if divergence is None else divergence + part_div
            state[0:ROWS] = rho - STEP * divergence
            for d in range(3):
                state[(1 + d) * ROWS : (2 + d) * ROWS] = field(flow, d) + STEP * (
                    -0.5 * grads[d] + 0.5 * field(laplace, d) + source[d * ROWS : (d + 1) * ROWS])
            state[4 * ROWS :] = field(flow, 3) + STEP * (
                -(2.0 / 3.0) * divergence + (2.0 / 3.0) * field(laplace, 3) + source[3 * ROWS :])
            return carry

        lax.fori_loop(0, MACRO_STEPS, sweep, 0)

    def coefficients(it):
        shift = target_ref[0, 0] - jnp.sum(mass[it]) / float(NX * NY * NZ * n_tx * n_ty)
        state[0:ROWS] = state[0:ROWS] + shift
        now = state[...]
        was = jnp.concatenate([gathered[it, c].reshape(ROWS, CELLS) for c in range(5)], axis=0)
        change = now - was
        fluid = wall_rows[0]

        def own(value):
            return value.reshape(5, 2, ROWS // 2, CELLS)[:, 0, NX : 2 * NX]

        def put(at, value):
            coef[at * 5 * NX : (at + 1) * 5 * NX, :] = (value * fluid[None]).reshape(5 * NX, CELLS)

        here = own(change)
        put(0, 0.9 * here + STEP * own(now))
        for at, shift_of in enumerate((x_last, x_next, y_last, y_next, z_last, z_next)):
            put(1 + at, own(shift_of(change)) - here)
        for x in range(NX):
            c = coef[pl.ds(x, COEF, stride=NX), :]
            c_high = rounded(c)
            coef3[x] = jnp.concatenate([c_high, c - c_high, c_high, jnp.zeros((8, CELLS), f32)], axis=0).astype(bf16)

    for it in range(ITERS):
        if it == 0:
            load.wait()
            for x in range(NX):
                part[pl.ds(x, 16, stride=NX), :] = projected(plane(0, x))
            greeted = n_vel - 1 + len(near_tiles)

            @pl.when(me == MASS)
            def _():
                pl.semaphore_wait(barrier, greeted + len(only_far))

            @pl.when(me != MASS)
            def _():
                pl.semaphore_wait(barrier, greeted)

        for step in range(1, n_vel):
            target, copy = rs_copy(it, step)
            pl.when(target <= MASS)(copy.start)

        if it > 0:
            def finalize(x, _, it=it):
                new = stream[x].reshape(CELLS, NV) + tn(coef3[x], rows3[...])
                h[it, x, 0:NY] = new.reshape(NY, NZ, NV)
                return 0

            lax.fori_loop(0, NX, finalize, 0)
        pack_edges(it)
        edges = edge_copies(it)
        for copy in edges:
            copy.start()

        @pl.when(me <= MASS)
        def _(it=it):
            total = part[pl.ds(pl.multiple_of(me * NX, NX), NX), :]
            for step in range(1, n_vel):
                rs_copy(it, step)[1].wait_recv()
            for step in range(1, n_vel):
                total = total + rs[it, step - 1]
            near[it, 1] = total

        @pl.when(me < NCOMP)
        def _(it=it):
            for copy in near_copies(it):
                copy.start()

        @pl.when(me == MASS)
        def _(it=it):
            for copy in tile_copies(it):
                copy.start()

        stream_inside(it)

        @pl.when(me < NCOMP)
        def _(it=it):
            for copy in near_copies(it):
                copy.wait_recv()
            for step in range(1, n_vel):
                all_copy(it, step).start()
            gathered[it, me] = near[it]

        @pl.when(me == MASS)
        def _(it=it):
            total = near[it, 1]
            for at, copy in enumerate(tile_copies(it)):
                copy.wait_recv()
                total = total + tile_mass[it, at]
            mass[it] = total
            for step in range(1, n_vel):
                mass_copy(it, step).start()

        for copy in edges:
            copy.wait_recv()
        stream_edges(it)
        if it + 1 < ITERS:
            for x in range(NX):
                stream_part[pl.ds(x, 16, stride=NX), :] = projected(stream[x].reshape(CELLS, NV))

        for c in range(NCOMP):
            @pl.when(me != c)
            def _(it=it, c=c):
                pltpu.make_async_remote_copy(
                    src_ref=near.at[it], dst_ref=gathered.at[it, c],
                    send_sem=all_send.at[it, 0], recv_sem=all_recv.at[it, c],
                    device_id=device(0, 0, group(1)), device_id_type=MESH).wait_recv()

        @pl.when(me != MASS)
        def _(it=it):
            mass_copy(it, 1).wait_recv()

        macro_solve(it)
        coefficients(it)

        for step in range(1, n_vel):
            target, copy = rs_copy(it, step)
            pl.when(target <= MASS)(copy.wait_send)
        if it + 1 < ITERS:
            for x in range(NX):
                at = pl.ds(x, 16, stride=NX)
                part[at, :] = stream_part[at, :] + jnp.dot(mixed3[...], coef3[x], preferred_element_type=f32)

    for x in range(NX):
        new = stream[x].reshape(CELLS, NV) + tn(coef3[x], rows3[...])
        dist_ref[x] = new.reshape(NY, NZ, NV)
    for k in range(5):
        value = state[k * ROWS + NX : k * ROWS + 2 * NX, :]
        for y in range(NY):
            moved = value if y == 0 else pltpu.roll(value, CELLS - y * NZ, 1)
            macro_ref[k, :, y, :] = moved[:, 0:NZ]

    for it in range(ITERS):
        for copy in edge_copies(it):
            copy.wait_send()

        @pl.when(me < NCOMP)
        def _(it=it):
            for copy in near_copies(it):
                copy.wait_send()
            for step in range(1, n_vel):
                all_copy(it, step).wait_send()

        @pl.when(me == MASS)
        def _(it=it):
            for copy in tile_copies(it):
                copy.wait_send()
            for step in range(1, n_vel):
                mass_copy(it, step).wait_send()


def on_device(sizes, initial, velocity, weights, wall, wall_temp, mass_target):
    n_tx, n_ty, n_vel = sizes
    dma = pltpu.SemaphoreType.DMA
    vmem = pl.BlockSpec(memory_space=pltpu.VMEM)
    tiles = n_tx * n_ty - 1
    return pl.pallas_call(
        functools.partial(kernel, sizes),
        out_shape=(jax.ShapeDtypeStruct((NX, NY, NZ, NV), f32), jax.ShapeDtypeStruct((5, NX, NY, NZ), f32)),
        in_specs=[pl.BlockSpec(memory_space=pl.ANY), vmem, vmem, vmem, vmem, pl.BlockSpec(memory_space=pltpu.SMEM)],
        out_specs=(vmem, vmem),
        scratch_shapes=[
            pltpu.VMEM((ITERS, NX + 1, NY + 1, NZ, NV), f32),
            pltpu.VMEM((NX, NY, NZ, NV), f32),
            pltpu.VMEM((ITERS, NX, NZ, NV), f32),
            pltpu.VMEM((16 * NX, CELLS), f32),
            pltpu.VMEM((16 * NX, CELLS), f32),
            pltpu.VMEM((ITERS, n_vel - 1, NX, CELLS), f32),
            pltpu.VMEM((ITERS, 6, NX, CELLS), f32),
            pltpu.VMEM((ITERS, NCOMP, 6, NX, CELLS), f32),
            pltpu.VMEM((ITERS, tiles, NX, CELLS), f32),
            pltpu.VMEM((ITERS, NX, CELLS), f32),
            pltpu.VMEM((COEF * NX, CELLS), f32),
            pltpu.VMEM((NX, 128, CELLS), bf16),
            pltpu.VMEM((128, NV), f32),
            pltpu.VMEM((128, NV), bf16),
            pltpu.VMEM((16, NV), f32),
            pltpu.VMEM((32, NV), bf16),
            pltpu.VMEM((16, 128), bf16),
            pltpu.VMEM((8, NV), f32),
            pltpu.VMEM((NX, CELLS, 128), f32),
            pltpu.VMEM((1, NX, CELLS), f32),
            pltpu.VMEM((5 * ROWS, CELLS), f32),
            pltpu.VMEM((4 * ROWS, CELLS), f32),
            dma,
            dma((ITERS, n_vel - 1)), dma((ITERS, n_vel - 1)),
            dma((ITERS, 5)), dma((ITERS, 6)),
            dma((ITERS, n_vel - 1)), dma((ITERS, NCOMP)),
            dma((ITERS, tiles)), dma((ITERS, tiles)),
            dma((ITERS, n_vel - 1)), dma((ITERS,)),
            dma((ITERS, 3)), dma((ITERS, 3)),
        ],
        compiler_params=pltpu.CompilerParams(collective_id=0, has_side_effects=True, vmem_limit_bytes=48 * 1024 * 1024),
    )(initial, velocity, weights.reshape(1, -1), wall, wall_temp, mass_target.reshape(1, 1))


def solution(mesh):
    sizes = (mesh.shape["tx"], mesh.shape["ty"], mesh.shape["vel"])
    placed = (
        P("tx", "ty", None, "vel"),
        P(None, "vel"),
        P("vel"),
        P("tx", "ty", None),
        P("tx", "ty", None),
        P(),
    )
    return jax.shard_map(
        functools.partial(on_device, sizes),
        mesh=mesh,
        in_specs=placed,
        out_specs=(P("tx", "ty", None, "vel"), P(None, "tx", "ty", None)),
        check_vma=False,
    )
```

```python
import functools

import jax
import jax.numpy as jnp
from jax import lax
from jax.experimental import pallas as pl
from jax.experimental.pallas import tpu as pltpu
from jax.sharding import PartitionSpec as P

ITERS = 3
MACRO_STEPS = 4
SETS = 4
DEPTH = (4, 3, 3, 3)
SLOTS = {0: (0, 0), 1: (0, 1), 2: (0, 2), 3: (0, 3), 4: (1, 0), 5: (1, 1), 6: (1, 2),
         8: (2, 0), 9: (2, 1), 10: (2, 2), 11: (3, 0), 12: (3, 1), 13: (3, 2)}
MASS = 3
STEP = 0.1
f32 = jnp.float32
bf16 = jnp.bfloat16
MESH = pl.DeviceIdType.MESH
NX, NY, NZ, NV = 8, 8, 16, 768
CELLS = NY * NZ
ROWS = 48
PACE = (3, 6)
REACH = 5
COEF = 40
NEIGHBOURS = [(0, -1), (0, 1), (1, -1), (1, 0), (1, 1)]


def nt(a, b, precision=None):
    return lax.dot_general(a, b, (((1,), (1,)), ((), ())), precision=precision, preferred_element_type=f32)


def tn(a, b):
    return lax.dot_general(a, b, (((0,), (0,)), ((), ())), preferred_element_type=f32)


def rounded(value):
    return value.astype(bf16).astype(f32)


def lanes_of(value):
    return lax.broadcasted_iota(jnp.int32, value.shape, 1)


def other_half(value):
    parts = value.reshape(-1, 2, ROWS // 2, CELLS)
    return jnp.concatenate([parts[:, 1:2], parts[:, 0:1]], axis=1).reshape(value.shape)


def x_next(v):
    return pltpu.roll(v, v.shape[0] - 1, 0)


def x_last(v):
    return pltpu.roll(v, 1, 0)


def y_next(v):
    r = pltpu.roll(v, CELLS - NZ, 1)
    return jnp.where(lanes_of(v) < CELLS - NZ, r, other_half(r))


def y_last(v):
    r = pltpu.roll(v, NZ, 1)
    return jnp.where(lanes_of(v) >= NZ, r, other_half(r))


def z_next(v):
    z = lax.rem(lanes_of(v), NZ)
    return jnp.where(z == NZ - 1, pltpu.roll(v, NZ - 1, 1), pltpu.roll(v, CELLS - 1, 1))


def z_last(v):
    z = lax.rem(lanes_of(v), NZ)
    return jnp.where(z == 0, pltpu.roll(v, CELLS - NZ + 1, 1), pltpu.roll(v, 1, 1))


def field(v, k):
    return v[k * ROWS : (k + 1) * ROWS]


def kernel(
    sizes,
    init_ref, vel_in, weight_in, wall_in, wall_temp_in, target_ref,
    dist_ref, macro_ref,
    h, stream, edge_y, part, stream_part, rs, halves, gathered, tile_mass, mass,
    coef, coef3, rows_f, rows3, proj_f, proj2, mixed3, factors, open_cells, wall_rows, state, source,
    vel_ref, weight_ref, wall_ref, wall_temp_ref,
    load_sem, small_sem, rs_send, rs_recv, half_send, half_recv, all_send, all_recv,
    tile_send, tile_recv, mass_send, mass_recv, edge_send, edge_recv,
):
    n_tx, n_ty, n_vel = sizes
    tx, ty, me = lax.axis_index("tx"), lax.axis_index("ty"), lax.axis_index("vel")
    high_bit, low_bit = lax.rem(me // 4, 2), lax.rem(me, 2)
    my_set = high_bit * 2 + low_bit
    base = me - high_bit * 4 - low_bit

    def device(dx, dy, vel):
        return {"tx": lax.rem(tx + (dx + n_tx), n_tx), "ty": lax.rem(ty + dy, n_ty), "vel": vel}

    middle_bit = lax.rem(me // 2, 2)
    across = me + 2 - 4 * middle_bit
    ring = n_vel // 2
    my_place = me // 4 * 2 + low_bit

    def place_of(step):
        return lax.rem(my_place + step, ring)

    def group(step):
        at = place_of(step)
        return at // 2 * 4 + middle_bit * 2 + lax.rem(at, 2)

    def set_of(vel):
        return lax.rem(vel // 4, 2) * 2 + lax.rem(vel, 2)

    def mate(a, b):
        return base + lax.rem(high_bit + a, 2) * 4 + lax.rem(low_bit + b, 2)

    mates = [(0, 1), (1, 0), (1, 1)]
    far_tiles = [(a, b) for b in range(n_ty) for a in range(n_tx) if (a, b) != (0, 0)]
    near_tiles = [(dx % n_tx, dy) for dy, dx in NEIGHBOURS]
    only_far = [t for t in far_tiles if t not in near_tiles]

    loads = [pltpu.make_async_copy(init_ref.at[x], h.at[0, x, 0:NY], load_sem.at[x]) for x in range(NX)]
    smalls = [pltpu.make_async_copy(a, b, small_sem.at[at]) for at, (a, b) in enumerate(
        ((vel_in, vel_ref), (weight_in, weight_ref), (wall_in, wall_ref), (wall_temp_in, wall_temp_ref)))]
    for copy in smalls + loads:
        copy.start()

    barrier = pltpu.get_barrier_semaphore()
    for step in range(1, ring):
        pl.semaphore_signal(barrier, inc=1, device_id=device(0, 0, group(step)), device_id_type=MESH)
    pl.semaphore_signal(barrier, inc=1, device_id=device(0, 0, across), device_id_type=MESH)
    for a, b in [(0, 0)] + mates:
        for dx, dy in near_tiles:
            pl.semaphore_signal(barrier, inc=1, device_id=device(dx, dy, mate(a, b)), device_id_type=MESH)

    @pl.when(my_set == MASS)
    def _():
        for a, b in only_far:
            pl.semaphore_signal(barrier, inc=1, device_id=device(a, b, me), device_id_type=MESH)

    smalls[0].wait()
    smalls[1].wait()

    vx, vy, vz = vel_ref[0:1, :], vel_ref[1:2, :], vel_ref[2:3, :]
    speed_sq = vx * vx + vy * vy + vz * vz
    ones = jnp.ones_like(vx)
    basis = [ones, 2.0 * vx, 2.0 * vy, 2.0 * vz, speed_sq - 1.5]
    sides = []
    for v in (vx, vy, vz):
        sides += [STEP * jnp.maximum(v, 0.0), -STEP * jnp.minimum(v, 0.0)]
    scale = weight_ref[0:1, :] / float(NV * n_vel)
    none = jnp.zeros_like(vx)
    moments = [ones, vx, vy, vz,
               (2.0 / 3.0) * speed_sq - 1.0, 2.0 * (vx * vx - speed_sq / 3.0), 2.0 * (vy * vy - speed_sq / 3.0), none,
               2.0 * vx * vy, 2.0 * vx * vz, 2.0 * vy * vz, none,
               vx * (speed_sq - 2.5), vy * (speed_sq - 2.5), vz * (speed_sq - 2.5), ones]
    for at, row in enumerate(moments):
        proj_f[at : at + 1, :] = row * scale
    proj = proj_f[...]
    proj2[...] = jnp.concatenate([rounded(proj), proj - rounded(proj)], axis=0).astype(bf16)

    def prepare():
        rows = basis + [side * b for side in sides for b in basis] + [basis[4]]
        for copy in range(3):
            for at, row in enumerate(rows):
                rows_f[copy * COEF + at : copy * COEF + at + 1, :] = row
            rows_f[copy * COEF + len(rows) : (copy + 1) * COEF, :] = jnp.zeros((COEF - len(rows), NV), f32)
        rows_f[3 * COEF :, :] = jnp.zeros((128 - 3 * COEF, NV), f32)
        bx, by, bz = (STEP * jnp.abs(v) for v in (vx, vy, vz))
        for at, row in enumerate((0.9 - bx - by - bz, bx, by, bz, vz)):
            factors[at : at + 1, :] = row
        every = rows_f[...]
        high = rounded(every)
        rows3[...] = jnp.where(lax.broadcasted_iota(jnp.int32, every.shape, 0) < 2 * COEF, high, every - high).astype(bf16)
        mixed = nt(proj_f[...], every, lax.Precision.HIGHEST)
        mixed_high = rounded(mixed)
        mixed3[...] = jnp.where(lanes_of(mixed) < 2 * COEF, mixed_high, mixed - mixed_high).astype(bf16)

        smalls[2].wait()
        smalls[3].wait()
        solid = jnp.zeros((NX, CELLS), f32)
        heat = jnp.zeros((NX, CELLS), f32)
        for y in range(NY):
            spread = (lax.broadcasted_iota(jnp.int32, (NZ, CELLS), 1)
                      == lax.broadcasted_iota(jnp.int32, (NZ, CELLS), 0) + y * NZ).astype(f32)
            is_wall = (wall_ref[:, y, :] == 1).astype(f32)
            solid = solid + lax.dot_general(is_wall, spread, (((1,), (0,)), ((), ())), precision=lax.Precision.HIGHEST,
                                            preferred_element_type=f32)
            heat = heat + lax.dot_general(is_wall * wall_temp_ref[:, y, :], spread, (((1,), (0,)), ((), ())),
                                          precision=lax.Precision.HIGHEST, preferred_element_type=f32)
        fluid = 1.0 - solid
        wall_rows[0] = fluid
        for x in range(NX):
            open_cells[x] = jnp.broadcast_to(fluid[x : x + 1], (CELLS, CELLS)).T
        coef[35 * NX : 36 * NX, :] = heat
        coef[36 * NX :, :] = jnp.zeros((4 * NX, CELLS), f32)

    def projected(value):
        top = value.astype(bf16)
        low = (value - top.astype(f32)).astype(bf16)
        both = nt(proj2[...], top)
        return both[0:16] + both[16:32] + nt(proj2[0:16, :], low)

    def plane(it, x):
        return h[it, x, 0:NY].reshape(CELLS, NV)

    def pack_edge(it, x):
        top, bottom = h[it, x, NY - 1], h[it, x, 0]
        for t in range(6):
            cut = slice(t * 128, (t + 1) * 128)
            if t in (0, 3):
                piece = top[:, cut]
            elif t in (2, 5):
                piece = bottom[:, cut]
            else:
                piece = jnp.where(lanes_of(top[:, cut]) < 64, top[:, cut], bottom[:, cut])
            edge_y[it, x, :, cut] = piece

    def ordered(at):
        return lax.rem(at * (NX - 1), NX)

    def y_copy(it, x):
        return pltpu.make_async_remote_copy(
            src_ref=edge_y.at[it, x], dst_ref=h.at[it, x, NY],
            send_sem=edge_send.at[it, x], recv_sem=edge_recv.at[it, x],
            device_id=device(0, 1, me), device_id_type=MESH)

    def x_copies(it):
        half = NV // 2
        return [
            pltpu.make_async_remote_copy(
                src_ref=h.at[it, 0, 0:NY, :, half:NV], dst_ref=h.at[it, NX, 0:NY, :, half:NV],
                send_sem=edge_send.at[it, NX], recv_sem=edge_recv.at[it, NX],
                device_id=device(-1, 0, me), device_id_type=MESH),
            pltpu.make_async_remote_copy(
                src_ref=h.at[it, NX - 1, 0:NY, :, 0:half], dst_ref=h.at[it, NX, 0:NY, :, 0:half],
                send_sem=edge_send.at[it, NX + 1], recv_sem=edge_recv.at[it, NX + 1],
                device_id=device(1, 0, me), device_id_type=MESH),
        ]

    def send_edges(it, fill):
        def body(at, _):
            x = ordered(at)
            fill(x)
            pack_edge(it, x)
            pl.when(at < PACE[0])(y_copy(it, x).start)
            return 0

        lax.fori_loop(0, 2, body, 0)
        for copy in x_copies(it):
            copy.start()
        lax.fori_loop(2, NX, body, 0)

    def send_more(it, first, last):
        def body(at, _):
            y_copy(it, ordered(at)).start()
            return 0

        lax.fori_loop(first, last, body, 0)

    def stream_cell(it, x, y):
        half = NV // 2
        x_down, x_up = lax.rem(x + NX, NX + 1), x + 1
        y_down, y_up = (y + NY) % (NY + 1), y + 1
        for t in range(6):
            cut = slice(t * 128, (t + 1) * 128)
            own = h[it, x, y, :, cut]
            from_x = h[it, x_down if t < 3 else x_up, y, :, cut]
            if t in (0, 3):
                from_y = h[it, x, y_down, :, cut]
            elif t in (2, 5):
                from_y = h[it, x, y_up, :, cut]
            else:
                from_y = jnp.where(lanes_of(own) < 64, h[it, x, y_down, :, cut], h[it, x, y_up, :, cut])
            up = jnp.broadcast_to(factors[4:5, cut], own.shape) > 0.0
            from_z = jnp.where(up, pltpu.roll(own, 1, 0), pltpu.roll(own, NZ - 1, 0))
            value = (factors[0:1, cut] * own + factors[1:2, cut] * from_x
                     + factors[2:3, cut] * from_y + factors[3:4, cut] * from_z)
            stream[x, y, :, cut] = value * open_cells[x, y * NZ : (y + 1) * NZ, :]

    def stream_inside(it):
        def body(x, _):
            for y in range(1, NY - 1):
                stream_cell(it, x, y)
            return 0

        lax.fori_loop(1, NX - 1, body, 0)

    def stream_ends(it):
        for copy in x_copies(it):
            copy.wait_recv()

        def body(side, _):
            for y in range(1, NY - 1):
                stream_cell(it, side * (NX - 1), y)
            return 0

        lax.fori_loop(0, 2, body, 0)

    def stream_sides(it):
        def body(at, _):
            x = ordered(at)
            y_copy(it, x).wait_recv()
            stream_cell(it, x, 0)
            stream_cell(it, x, NY - 1)
            if it + 1 < ITERS:
                stream_part[pl.ds(x, 16, stride=NX), :] = projected(stream[x].reshape(CELLS, NV))
            return 0

        lax.fori_loop(0, NX, body, 0)

    def rs_copy(it, step):
        target = group(step)
        return pltpu.make_async_remote_copy(
            src_ref=part.at[pl.ds(pl.multiple_of(set_of(target) * 4 * NX, 4 * NX), 4 * NX)], dst_ref=rs.at[it, my_place],
            send_sem=rs_send.at[it, step - 1], recv_sem=rs_recv.at[it, my_place],
            device_id=device(0, 0, target), device_id_type=MESH)

    def rs_wait(it, step):
        at = place_of(step)
        pltpu.make_async_remote_copy(
            src_ref=part.at[0 : 4 * NX], dst_ref=rs.at[it, at],
            send_sem=rs_send.at[it, step - 1], recv_sem=rs_recv.at[it, at],
            device_id=device(0, 0, group(step)), device_id_type=MESH).wait_recv()

    def half_copy(it):
        return pltpu.make_async_remote_copy(
            src_ref=halves.at[it, 0], dst_ref=halves.at[it, 1],
            send_sem=half_send.at[it], recv_sem=half_recv.at[it],
            device_id=device(0, 0, across), device_id_type=MESH)

    def all_copies(it, depth):
        copies = []
        for a, b in [(0, 0)] + mates:
            for dy, dx in [(0, 0)] + NEIGHBOURS:
                if (a, b, dx, dy) == (0, 0, 0, 0):
                    continue
                slot = dy * 3 + 1 - dx
                cut = slice(0, 8) if dx == 0 else slice(8 - REACH, 8) if dx == 1 else slice(0, REACH)
                copies.append(pltpu.make_async_remote_copy(
                    src_ref=gathered.at[it, my_set, 1, 0:depth, cut], dst_ref=gathered.at[it, my_set, slot, 0:depth, cut],
                    send_sem=all_send.at[it, len(copies)], recv_sem=all_recv.at[it, my_set, slot],
                    device_id=device(dx, dy, mate(a, b)), device_id_type=MESH))
        return copies

    def for_depth(action):
        for depth in sorted(set(DEPTH)):
            wanted = [at for at in range(SETS) if DEPTH[at] == depth]
            match = my_set == wanted[0]
            for at in wanted[1:]:
                match = jnp.logical_or(match, my_set == at)

            @pl.when(match)
            def _(depth=depth):
                action(depth)

    def wait_all(it):
        for at in range(SETS):
            for slot in range(6):
                dx = 1 - slot % 3
                cut = slice(0, 8) if dx == 0 else slice(8 - REACH, 8) if dx == 1 else slice(0, REACH)

                def wait(at=at, slot=slot, cut=cut):
                    pltpu.make_async_remote_copy(
                        src_ref=gathered.at[it, at, 1, 0 : DEPTH[at], cut],
                        dst_ref=gathered.at[it, at, slot, 0 : DEPTH[at], cut],
                        send_sem=all_send.at[it, 0], recv_sem=all_recv.at[it, at, slot],
                        device_id=device(0, 0, group(1)), device_id_type=MESH).wait_recv()

                if slot == 1:
                    pl.when(my_set != at)(wait)
                else:
                    wait()

    def tile_copies(it):
        return [
            pltpu.make_async_remote_copy(
                src_ref=gathered.at[it, my_set, 1, 3], dst_ref=tile_mass.at[it, at],
                send_sem=tile_send.at[it, at], recv_sem=tile_recv.at[it, at],
                device_id=device(a, b, me), device_id_type=MESH)
            for at, (a, b) in enumerate(far_tiles)
        ]

    def mass_copies(it):
        return [
            pltpu.make_async_remote_copy(
                src_ref=mass.at[it], dst_ref=mass.at[it],
                send_sem=mass_send.at[it, at], recv_sem=mass_recv.at[it],
                device_id=device(0, 0, mate(a, b)), device_id_type=MESH)
            for at, (a, b) in enumerate(mates)
        ]

    def macro_solve(it):
        def g(c):
            if c == 7:
                return -(g(5) + g(6))
            at, k = SLOTS[c]
            return gathered[it, at, :, k].reshape(ROWS, CELLS)

        def many(*cs):
            return jnp.concatenate([g(c) for c in cs], axis=0)

        flow = many(1, 2, 3, 4)
        along = (many(5, 8, 9, 11), many(8, 6, 10, 12), many(9, 10, 7, 13))
        shifts = ((x_next, x_last), (y_next, y_last), (z_next, z_last))
        total = -6.0 * flow
        for (after, before), a in zip(shifts, along):
            total = total + (after(flow + 0.5 * a) + before(flow - 0.5 * a))
        source[0 : 3 * ROWS] = -0.5 * total[0 : 3 * ROWS]
        source[3 * ROWS :] = -(2.0 / 3.0) * total[3 * ROWS :]
        state[...] = many(0, 1, 2, 3, 4)

        def sweep(_, carry):
            rho, flow = state[0:ROWS], state[ROWS : 5 * ROWS]
            stack = jnp.concatenate([rho + field(flow, 3), flow], axis=0)
            laplace = -6.0 * flow
            grads, divergence = [], None
            for d, (after, before) in enumerate(shifts):
                up, down = after(stack), before(stack)
                laplace = laplace + (up[ROWS:] + down[ROWS:])
                grads.append(0.5 * (field(up, 0) - field(down, 0)))
                part_div = 0.5 * (field(up, 1 + d) - field(down, 1 + d))
                divergence = part_div if divergence is None else divergence + part_div
            state[0:ROWS] = rho - STEP * divergence
            for d in range(3):
                state[(1 + d) * ROWS : (2 + d) * ROWS] = field(flow, d) + STEP * (
                    -0.5 * grads[d] + 0.5 * field(laplace, d) + source[d * ROWS : (d + 1) * ROWS])
            state[4 * ROWS :] = field(flow, 3) + STEP * (
                -(2.0 / 3.0) * divergence + (2.0 / 3.0) * field(laplace, 3) + source[3 * ROWS :])
            return carry

        lax.fori_loop(0, MACRO_STEPS, sweep, 0)

    def coefficients(it):
        shift = target_ref[0, 0] - jnp.sum(mass[it]) / float(NX * NY * NZ * n_tx * n_ty)
        state[0:ROWS] = state[0:ROWS] + shift
        now = state[...]
        was = jnp.concatenate([gathered[it, SLOTS[c][0], :, SLOTS[c][1]].reshape(ROWS, CELLS) for c in range(5)], axis=0)
        change = now - was
        fluid = wall_rows[0]

        def own(value):
            return value.reshape(5, 2, ROWS // 2, CELLS)[:, 0, NX : 2 * NX]

        def put(at, value):
            coef[at * 5 * NX : (at + 1) * 5 * NX, :] = (value * fluid[None]).reshape(5 * NX, CELLS)

        here = own(change)
        put(0, 0.9 * here + STEP * own(now))
        for at, shift_of in enumerate((x_last, x_next, y_last, y_next, z_last, z_next)):
            put(1 + at, own(shift_of(change)) - here)
        for x in range(NX):
            c = coef[pl.ds(x, COEF, stride=NX), :]
            c_high = rounded(c)
            coef3[x] = jnp.concatenate([c_high, c - c_high, c_high, jnp.zeros((8, CELLS), f32)], axis=0).astype(bf16)

    def place(it, x, value):
        part[pl.ds(x, 16, stride=NX), :] = value

    for it in range(ITERS):
        if it == 0:
            for x in range(NX):
                loads[x].wait()
                place(0, x, projected(plane(0, x)))
            greeted = ring + 4 * len(near_tiles)

            @pl.when(my_set == MASS)
            def _():
                pl.semaphore_wait(barrier, greeted + len(only_far))

            @pl.when(my_set != MASS)
            def _():
                pl.semaphore_wait(barrier, greeted)

        for step in range(1, ring):
            rs_copy(it, step).start()

        def finalize(x, it=it):
            if it > 0:
                new = stream[x].reshape(CELLS, NV) + tn(coef3[x], rows3[...])
                h[it, x, 0:NY] = new.reshape(NY, NZ, NV)

        send_edges(it, finalize)
        if it == 0:
            prepare()

        rs[it, my_place] = part[pl.ds(pl.multiple_of(my_set * 4 * NX, 4 * NX), 4 * NX), :]
        for step in range(1, ring):
            rs_wait(it, step)
        total = rs[it, 0]
        for at in range(1, ring):
            total = total + rs[it, at]
        halves[it, 0] = total
        half_copy(it).start()
        send_more(it, PACE[0], PACE[1])
        stream_inside(it)
        half_copy(it).wait_recv()
        gathered[it, my_set, 1] = (total + halves[it, 1]).reshape(4, NX, CELLS)

        @pl.when(my_set == MASS)
        def _(it=it):
            for copy in tile_copies(it):
                copy.start()

        def send_all(depth, it=it):
            for copy in all_copies(it, depth):
                copy.start()

        for_depth(send_all)
        send_more(it, PACE[1], NX)

        @pl.when(my_set == MASS)
        def _(it=it):
            total = gathered[it, my_set, 1, 3]
            for at, copy in enumerate(tile_copies(it)):
                copy.wait_recv()
                total = total + tile_mass[it, at]
            mass[it] = total
            for copy in mass_copies(it):
                copy.start()

        stream_ends(it)
        stream_sides(it)
        wait_all(it)
        macro_solve(it)

        @pl.when(my_set != MASS)
        def _(it=it):
            mass_copies(it)[0].wait_recv()

        coefficients(it)

        for step in range(1, ring):
            rs_copy(it, step).wait_send()
        if it + 1 < ITERS:
            for x in range(NX):
                at = pl.ds(x, 16, stride=NX)
                part[at, :] = stream_part[at, :] + jnp.dot(mixed3[...], coef3[x], preferred_element_type=f32)

    for x in range(NX):
        new = stream[x].reshape(CELLS, NV) + tn(coef3[x], rows3[...])
        dist_ref[x] = new.reshape(NY, NZ, NV)
    for k in range(5):
        value = state[k * ROWS + NX : k * ROWS + 2 * NX, :]
        for y in range(NY):
            moved = value if y == 0 else pltpu.roll(value, CELLS - y * NZ, 1)
            macro_ref[k, :, y, :] = moved[:, 0:NZ]

    for it in range(ITERS):
        half_copy(it).wait_send()
        for copy in x_copies(it):
            copy.wait_send()

        def sent(x, _, it=it):
            y_copy(it, x).wait_send()
            return 0

        lax.fori_loop(0, NX, sent, 0)

        def sent_all(depth, it=it):
            for copy in all_copies(it, depth):
                copy.wait_send()

        for_depth(sent_all)

        @pl.when(my_set == MASS)
        def _(it=it):
            for copy in tile_copies(it):
                copy.wait_send()
            for copy in mass_copies(it):
                copy.wait_send()


def on_device(sizes, initial, velocity, weights, wall, wall_temp, mass_target):
    n_tx, n_ty, n_vel = sizes
    dma = pltpu.SemaphoreType.DMA
    vmem = pl.BlockSpec(memory_space=pltpu.VMEM)
    tiles = n_tx * n_ty - 1
    return pl.pallas_call(
        functools.partial(kernel, sizes),
        out_shape=(jax.ShapeDtypeStruct((NX, NY, NZ, NV), f32), jax.ShapeDtypeStruct((5, NX, NY, NZ), f32)),
        in_specs=[pl.BlockSpec(memory_space=pltpu.HBM)] * 5 + [pl.BlockSpec(memory_space=pltpu.SMEM)],
        out_specs=(vmem, vmem),
        scratch_shapes=[
            pltpu.VMEM((ITERS, NX + 1, NY + 1, NZ, NV), f32),
            pltpu.VMEM((NX, NY, NZ, NV), f32),
            pltpu.VMEM((ITERS, NX, NZ, NV), f32),
            pltpu.VMEM((16 * NX, CELLS), f32),
            pltpu.VMEM((16 * NX, CELLS), f32),
            pltpu.VMEM((ITERS, n_vel // 2, 4 * NX, CELLS), f32),
            pltpu.VMEM((ITERS, 2, 4 * NX, CELLS), f32),
            pltpu.VMEM((ITERS, SETS, 6, 4, NX, CELLS), f32),
            pltpu.VMEM((ITERS, tiles, NX, CELLS), f32),
            pltpu.VMEM((ITERS, NX, CELLS), f32),
            pltpu.VMEM((COEF * NX, CELLS), f32),
            pltpu.VMEM((NX, 128, CELLS), bf16),
            pltpu.VMEM((128, NV), f32),
            pltpu.VMEM((128, NV), bf16),
            pltpu.VMEM((16, NV), f32),
            pltpu.VMEM((32, NV), bf16),
            pltpu.VMEM((16, 128), bf16),
            pltpu.VMEM((8, NV), f32),
            pltpu.VMEM((NX, CELLS, 128), f32),
            pltpu.VMEM((1, NX, CELLS), f32),
            pltpu.VMEM((5 * ROWS, CELLS), f32),
            pltpu.VMEM((4 * ROWS, CELLS), f32),
            pltpu.VMEM((3, NV), f32), pltpu.VMEM((1, NV), f32),
            pltpu.VMEM((NX, NY, NZ), jnp.int32), pltpu.VMEM((NX, NY, NZ), f32),
            dma((NX,)), dma((4,)),
            dma((ITERS, n_vel // 2 - 1)), dma((ITERS, n_vel // 2)),
            dma((ITERS,)), dma((ITERS,)),
            dma((ITERS, 23)), dma((ITERS, SETS, 6)),
            dma((ITERS, tiles)), dma((ITERS, tiles)),
            dma((ITERS, 3)), dma((ITERS,)),
            dma((ITERS, NX + 2)), dma((ITERS, NX + 2)),
        ],
        compiler_params=pltpu.CompilerParams(collective_id=0, has_side_effects=True, vmem_limit_bytes=48 * 1024 * 1024),
    )(initial, velocity, weights.reshape(1, -1), wall, wall_temp, mass_target.reshape(1, 1))


def solution(mesh):
    sizes = (mesh.shape["tx"], mesh.shape["ty"], mesh.shape["vel"])
    placed = (
        P("tx", "ty", None, "vel"),
        P(None, "vel"),
        P("vel"),
        P("tx", "ty", None),
        P("tx", "ty", None),
        P(),
    )
    return jax.shard_map(
        functools.partial(on_device, sizes),
        mesh=mesh,
        in_specs=placed,
        out_specs=(P("tx", "ty", None, "vel"), P(None, "tx", "ty", None)),
        check_vma=False,
    )
```

```python
import functools

import jax
import jax.numpy as jnp
from jax import lax
from jax.experimental import pallas as pl
from jax.experimental.pallas import tpu as pltpu
from jax.sharding import PartitionSpec as P

ITERS = 3
MACRO_STEPS = 4
SETS = 4
DEPTH = (4, 3, 3, 3)
SLOTS = {0: (0, 0), 1: (0, 1), 2: (0, 2), 3: (0, 3), 4: (1, 0), 5: (1, 1), 6: (1, 2),
         8: (2, 0), 9: (2, 1), 10: (2, 2), 11: (3, 0), 12: (3, 1), 13: (3, 2)}
MASS = 3
STEP = 0.1
f32 = jnp.float32
bf16 = jnp.bfloat16
MESH = pl.DeviceIdType.MESH
NX, NY, NZ, NV = 8, 8, 16, 768
CELLS = NY * NZ
ROWS = 48
PACE = (4, 7)
EARLY = 6
REACH = 5
COEF = 40
FAR_FIRST = [(1, -1), (1, 1), (0, -1), (0, 1), (1, 0), (0, 0)]
NEIGHBOURS = [(0, -1), (0, 1), (1, -1), (1, 0), (1, 1)]


def nt(a, b, precision=None):
    return lax.dot_general(a, b, (((1,), (1,)), ((), ())), precision=precision, preferred_element_type=f32)


def tn(a, b):
    return lax.dot_general(a, b, (((0,), (0,)), ((), ())), preferred_element_type=f32)


def rounded(value):
    return value.astype(bf16).astype(f32)


def lanes_of(value):
    return lax.broadcasted_iota(jnp.int32, value.shape, 1)


def other_half(value):
    parts = value.reshape(-1, 2, ROWS // 2, CELLS)
    return jnp.concatenate([parts[:, 1:2], parts[:, 0:1]], axis=1).reshape(value.shape)


def x_next(v):
    return pltpu.roll(v, v.shape[0] - 1, 0)


def x_last(v):
    return pltpu.roll(v, 1, 0)


def y_next(v):
    r = pltpu.roll(v, CELLS - NZ, 1)
    return jnp.where(lanes_of(v) < CELLS - NZ, r, other_half(r))


def y_last(v):
    r = pltpu.roll(v, NZ, 1)
    return jnp.where(lanes_of(v) >= NZ, r, other_half(r))


def z_next(v):
    z = lax.rem(lanes_of(v), NZ)
    return jnp.where(z == NZ - 1, pltpu.roll(v, NZ - 1, 1), pltpu.roll(v, CELLS - 1, 1))


def z_last(v):
    z = lax.rem(lanes_of(v), NZ)
    return jnp.where(z == 0, pltpu.roll(v, CELLS - NZ + 1, 1), pltpu.roll(v, 1, 1))


def field(v, k):
    return v[k * ROWS : (k + 1) * ROWS]


def kernel(
    sizes,
    init_ref, vel_in, weight_in, wall_in, wall_temp_in, target_ref,
    dist_ref, macro_ref,
    h, stream, edge_y, part, stream_part, rs, halves, gathered, tile_mass, mass,
    coef, coef3, rows_f, rows3, proj_f, proj2, mixed3, factors, open_cells, wall_rows, state, source,
    velocity_ref, weight_ref, wall_ref, wall_temp_ref,
    load_sem, small_sem, rs_send, rs_recv, half_send, half_recv, all_send, all_recv,
    tile_send, tile_recv, mass_send, mass_recv, edge_send, edge_recv,
):
    n_tx, n_ty, n_vel = sizes
    tx, ty, me = lax.axis_index("tx"), lax.axis_index("ty"), lax.axis_index("vel")
    high_bit, low_bit = lax.rem(me // 4, 2), lax.rem(me, 2)
    my_set = high_bit * 2 + low_bit
    base = me - high_bit * 4 - low_bit

    def device(dx, dy, vel):
        return {"tx": lax.rem(tx + (dx + n_tx), n_tx), "ty": lax.rem(ty + dy, n_ty), "vel": vel}

    middle_bit = lax.rem(me // 2, 2)
    across = me + 2 - 4 * middle_bit
    ring = n_vel // 2
    my_place = me // 4 * 2 + low_bit

    def place_of(step):
        return lax.rem(my_place + step, ring)

    def group(step):
        at = place_of(step)
        return at // 2 * 4 + middle_bit * 2 + lax.rem(at, 2)

    def set_of(vel):
        return lax.rem(vel // 4, 2) * 2 + lax.rem(vel, 2)

    def mate(a, b):
        return base + lax.rem(high_bit + a, 2) * 4 + lax.rem(low_bit + b, 2)

    mates = [(0, 1), (1, 0), (1, 1)]
    far_tiles = [(a, b) for b in range(n_ty) for a in range(n_tx) if (a, b) != (0, 0)]
    near_tiles = [(dx % n_tx, dy) for dy, dx in NEIGHBOURS]
    only_far = [t for t in far_tiles if t not in near_tiles]

    loads = [pltpu.make_async_copy(init_ref.at[x], h.at[0, x, 0:NY], load_sem.at[x]) for x in range(NX)]
    smalls = [pltpu.make_async_copy(a, b, small_sem.at[at]) for at, (a, b) in enumerate(
        ((vel_in, velocity_ref), (weight_in, weight_ref), (wall_in, wall_ref), (wall_temp_in, wall_temp_ref)))]
    for copy in smalls + loads:
        copy.start()

    barrier = pltpu.get_barrier_semaphore()
    for step in range(1, ring):
        pl.semaphore_signal(barrier, inc=1, device_id=device(0, 0, group(step)), device_id_type=MESH)
    pl.semaphore_signal(barrier, inc=1, device_id=device(0, 0, across), device_id_type=MESH)
    for a, b in [(0, 0)] + mates:
        for dx, dy in near_tiles:
            pl.semaphore_signal(barrier, inc=1, device_id=device(dx, dy, mate(a, b)), device_id_type=MESH)

    @pl.when(my_set == MASS)
    def _():
        for a, b in only_far:
            pl.semaphore_signal(barrier, inc=1, device_id=device(a, b, me), device_id_type=MESH)

    smalls[0].wait()
    smalls[1].wait()
    vx, vy, vz = velocity_ref[0:1, :], velocity_ref[1:2, :], velocity_ref[2:3, :]
    speed_sq = vx * vx + vy * vy + vz * vz
    ones = jnp.ones_like(vx)
    basis = [ones, 2.0 * vx, 2.0 * vy, 2.0 * vz, speed_sq - 1.5]
    sides = []
    for v in (vx, vy, vz):
        sides += [STEP * jnp.maximum(v, 0.0), -STEP * jnp.minimum(v, 0.0)]
    scale = weight_ref[...].reshape(1, NV) / float(NV * n_vel)
    none = jnp.zeros_like(vx)
    moments = [ones, vx, vy, vz,
               (2.0 / 3.0) * speed_sq - 1.0, 2.0 * (vx * vx - speed_sq / 3.0), 2.0 * (vy * vy - speed_sq / 3.0), none,
               2.0 * vx * vy, 2.0 * vx * vz, 2.0 * vy * vz, none,
               vx * (speed_sq - 2.5), vy * (speed_sq - 2.5), vz * (speed_sq - 2.5), ones]
    for at, row in enumerate(moments):
        proj_f[at : at + 1, :] = row * scale
    proj = proj_f[...]
    proj2[...] = jnp.concatenate([rounded(proj), proj - rounded(proj)], axis=0).astype(bf16)

    def prepare():
        bx, by, bz = (STEP * jnp.abs(v) for v in (vx, vy, vz))
        for at, row in enumerate((0.9 - bx - by - bz, bx, by, bz, vz)):
            factors[at : at + 1, :] = row
        smalls[2].wait()
        smalls[3].wait()
        solid = jnp.zeros((NX, CELLS), f32)
        heat = jnp.zeros((NX, CELLS), f32)
        for y in range(NY):
            spread = (lax.broadcasted_iota(jnp.int32, (NZ, CELLS), 1)
                      == lax.broadcasted_iota(jnp.int32, (NZ, CELLS), 0) + y * NZ).astype(f32)
            is_wall = (wall_ref[:, y, :] == 1).astype(f32)
            both = jnp.concatenate([is_wall, is_wall * wall_temp_ref[:, y, :]], axis=0)
            moved = lax.dot_general(both, spread, (((1,), (0,)), ((), ())), precision=lax.Precision.HIGHEST,
                                    preferred_element_type=f32)
            solid = solid + moved[0:NX]
            heat = heat + moved[NX:]
        fluid = 1.0 - solid
        wall_rows[0] = fluid
        for x in range(NX):
            open_cells[x] = jnp.broadcast_to(fluid[x : x + 1], (CELLS, CELLS)).T
        coef[35 * NX : 36 * NX, :] = heat
        coef[36 * NX :, :] = jnp.zeros((4 * NX, CELLS), f32)

    def prepare_rows():
        rows = basis + [side * b for side in sides for b in basis] + [basis[4]]
        for copy in range(3):
            for at, row in enumerate(rows):
                rows_f[copy * COEF + at : copy * COEF + at + 1, :] = row
            rows_f[copy * COEF + len(rows) : (copy + 1) * COEF, :] = jnp.zeros((COEF - len(rows), NV), f32)
        rows_f[3 * COEF :, :] = jnp.zeros((128 - 3 * COEF, NV), f32)
        every = rows_f[...]
        high = rounded(every)
        rows3[...] = jnp.where(lax.broadcasted_iota(jnp.int32, every.shape, 0) < 2 * COEF, high, every - high).astype(bf16)
        mixed = nt(proj_f[...], every, lax.Precision.HIGHEST)
        mixed_high = rounded(mixed)
        mixed3[...] = jnp.where(lanes_of(mixed) < 2 * COEF, mixed_high, mixed - mixed_high).astype(bf16)

    def projected(value):
        top = value.astype(bf16)
        low = (value - top.astype(f32)).astype(bf16)
        both = nt(proj2[...], top)
        return both[0:16] + both[16:32] + nt(proj2[0:16, :], low)

    def plane(it, x):
        return h[it, x, 0:NY].reshape(CELLS, NV)

    def pack_edge(it, x):
        top, bottom = h[it, x, NY - 1], h[it, x, 0]
        for t in range(6):
            cut = slice(t * 128, (t + 1) * 128)
            if t in (0, 3):
                piece = top[:, cut]
            elif t in (2, 5):
                piece = bottom[:, cut]
            else:
                piece = jnp.where(lanes_of(top[:, cut]) < 64, top[:, cut], bottom[:, cut])
            edge_y[it, x, :, cut] = piece

    def ordered(at):
        return lax.rem(at * (NX - 1), NX)

    def y_copy(it, x):
        return pltpu.make_async_remote_copy(
            src_ref=edge_y.at[it, x], dst_ref=h.at[it, x, NY],
            send_sem=edge_send.at[it, x], recv_sem=edge_recv.at[it, x],
            device_id=device(0, 1, me), device_id_type=MESH)

    def x_copies(it):
        half = NV // 2
        return [
            pltpu.make_async_remote_copy(
                src_ref=h.at[it, 0, 0:NY, :, half:NV], dst_ref=h.at[it, NX, 0:NY, :, half:NV],
                send_sem=edge_send.at[it, NX], recv_sem=edge_recv.at[it, NX],
                device_id=device(-1, 0, me), device_id_type=MESH),
            pltpu.make_async_remote_copy(
                src_ref=h.at[it, NX - 1, 0:NY, :, 0:half], dst_ref=h.at[it, NX, 0:NY, :, 0:half],
                send_sem=edge_send.at[it, NX + 1], recv_sem=edge_recv.at[it, NX + 1],
                device_id=device(1, 0, me), device_id_type=MESH),
        ]

    def send_edges(it, fill):
        def body(at, _):
            x = ordered(at)
            fill(x)
            pack_edge(it, x)
            pl.when(at < PACE[0])(y_copy(it, x).start)
            return 0

        lax.fori_loop(0, 2, body, 0)
        for copy in x_copies(it):
            copy.start()
        lax.fori_loop(2, NX, body, 0)

    def send_more(it, first, last):
        def body(at, _):
            y_copy(it, ordered(at)).start()
            return 0

        lax.fori_loop(first, last, body, 0)

    def stream_cell(it, x, y):
        half = NV // 2
        x_down, x_up = lax.rem(x + NX, NX + 1), x + 1
        y_down, y_up = (y + NY) % (NY + 1), y + 1
        for t in range(6):
            cut = slice(t * 128, (t + 1) * 128)
            own = h[it, x, y, :, cut]
            from_x = h[it, x_down if t < 3 else x_up, y, :, cut]
            if t in (0, 3):
                from_y = h[it, x, y_down, :, cut]
            elif t in (2, 5):
                from_y = h[it, x, y_up, :, cut]
            else:
                from_y = jnp.where(lanes_of(own) < 64, h[it, x, y_down, :, cut], h[it, x, y_up, :, cut])
            up = jnp.broadcast_to(factors[4:5, cut], own.shape) > 0.0
            from_z = jnp.where(up, pltpu.roll(own, 1, 0), pltpu.roll(own, NZ - 1, 0))
            value = (factors[0:1, cut] * own + factors[1:2, cut] * from_x
                     + factors[2:3, cut] * from_y + factors[3:4, cut] * from_z)
            stream[x, y, :, cut] = value * open_cells[x, y * NZ : (y + 1) * NZ, :]

    def stream_inside(it):
        def body(x, _):
            for y in range(1, NY - 1):
                stream_cell(it, x, y)
            return 0

        lax.fori_loop(1, NX - 1, body, 0)

    def stream_ends(it):
        for copy in x_copies(it):
            copy.wait_recv()

        def body(side, _):
            for y in range(1, NY - 1):
                stream_cell(it, side * (NX - 1), y)
            return 0

        lax.fori_loop(0, 2, body, 0)

    def stream_sides(it, first, last):
        def body(at, _):
            x = ordered(at)
            y_copy(it, x).wait_recv()
            stream_cell(it, x, 0)
            stream_cell(it, x, NY - 1)
            if it + 1 < ITERS:
                stream_part[pl.ds(x, 16, stride=NX), :] = projected(stream[x].reshape(CELLS, NV))
            return 0

        lax.fori_loop(first, last, body, 0)

    def rs_copy(it, step):
        target = group(step)
        return pltpu.make_async_remote_copy(
            src_ref=part.at[pl.ds(pl.multiple_of(set_of(target) * 4 * NX, 4 * NX), 4 * NX)], dst_ref=rs.at[it, my_place],
            send_sem=rs_send.at[it, step - 1], recv_sem=rs_recv.at[it, my_place],
            device_id=device(0, 0, target), device_id_type=MESH)

    def rs_wait(it, step):
        at = place_of(step)
        pltpu.make_async_remote_copy(
            src_ref=part.at[0 : 4 * NX], dst_ref=rs.at[it, at],
            send_sem=rs_send.at[it, step - 1], recv_sem=rs_recv.at[it, at],
            device_id=device(0, 0, group(step)), device_id_type=MESH).wait_recv()

    def half_copy(it):
        return pltpu.make_async_remote_copy(
            src_ref=halves.at[it, 0], dst_ref=halves.at[it, 1],
            send_sem=half_send.at[it], recv_sem=half_recv.at[it],
            device_id=device(0, 0, across), device_id_type=MESH)

    def all_copies(it, depth):
        copies = []
        for dy, dx in FAR_FIRST:
            for a, b in mates[::-1] + [(0, 0)]:
                if (a, b, dx, dy) == (0, 0, 0, 0):
                    continue
                slot = dy * 3 + 1 - dx
                cut = slice(0, 8) if dx == 0 else slice(8 - REACH, 8) if dx == 1 else slice(0, REACH)
                copies.append(pltpu.make_async_remote_copy(
                    src_ref=gathered.at[it, my_set, 1, 0:depth, cut], dst_ref=gathered.at[it, my_set, slot, 0:depth, cut],
                    send_sem=all_send.at[it, len(copies)], recv_sem=all_recv.at[it, my_set, slot],
                    device_id=device(dx, dy, mate(a, b)), device_id_type=MESH))
        return copies

    def for_depth(action):
        for depth in sorted(set(DEPTH)):
            wanted = [at for at in range(SETS) if DEPTH[at] == depth]
            match = my_set == wanted[0]
            for at in wanted[1:]:
                match = jnp.logical_or(match, my_set == at)

            @pl.when(match)
            def _(depth=depth):
                action(depth)

    def wait_all(it):
        for at in range(SETS):
            for slot in range(6):
                dx = 1 - slot % 3
                cut = slice(0, 8) if dx == 0 else slice(8 - REACH, 8) if dx == 1 else slice(0, REACH)

                def wait(at=at, slot=slot, cut=cut):
                    pltpu.make_async_remote_copy(
                        src_ref=gathered.at[it, at, 1, 0 : DEPTH[at], cut],
                        dst_ref=gathered.at[it, at, slot, 0 : DEPTH[at], cut],
                        send_sem=all_send.at[it, 0], recv_sem=all_recv.at[it, at, slot],
                        device_id=device(0, 0, group(1)), device_id_type=MESH).wait_recv()

                if slot == 1:
                    pl.when(my_set != at)(wait)
                else:
                    wait()

    def tile_copies(it):
        return [
            pltpu.make_async_remote_copy(
                src_ref=gathered.at[it, my_set, 1, 3], dst_ref=tile_mass.at[it, at],
                send_sem=tile_send.at[it, at], recv_sem=tile_recv.at[it, at],
                device_id=device(a, b, me), device_id_type=MESH)
            for at, (a, b) in enumerate(far_tiles)
        ]

    def mass_copies(it):
        return [
            pltpu.make_async_remote_copy(
                src_ref=mass.at[it], dst_ref=mass.at[it],
                send_sem=mass_send.at[it, at], recv_sem=mass_recv.at[it],
                device_id=device(0, 0, mate(a, b)), device_id_type=MESH)
            for at, (a, b) in enumerate(mates)
        ]

    def macro_solve(it):
        def g(c):
            if c == 7:
                return -(g(5) + g(6))
            at, k = SLOTS[c]
            return gathered[it, at, :, k].reshape(ROWS, CELLS)

        def many(*cs):
            return jnp.concatenate([g(c) for c in cs], axis=0)

        flow = many(1, 2, 3, 4)
        along = (many(5, 8, 9, 11), many(8, 6, 10, 12), many(9, 10, 7, 13))
        shifts = ((x_next, x_last), (y_next, y_last), (z_next, z_last))
        total = -6.0 * flow
        for (after, before), a in zip(shifts, along):
            total = total + (after(flow + 0.5 * a) + before(flow - 0.5 * a))
        source[0 : 3 * ROWS] = -0.5 * total[0 : 3 * ROWS]
        source[3 * ROWS :] = -(2.0 / 3.0) * total[3 * ROWS :]
        state[...] = many(0, 1, 2, 3, 4)

        def sweep(_, carry):
            rho, flow = state[0:ROWS], state[ROWS : 5 * ROWS]
            stack = jnp.concatenate([rho + field(flow, 3), flow], axis=0)
            laplace = -6.0 * flow
            grads, divergence = [], None
            for d, (after, before) in enumerate(shifts):
                up, down = after(stack), before(stack)
                laplace = laplace + (up[ROWS:] + down[ROWS:])
                grads.append(0.5 * (field(up, 0) - field(down, 0)))
                part_div = 0.5 * (field(up, 1 + d) - field(down, 1 + d))
                divergence = part_div if divergence is None else divergence + part_div
            state[0:ROWS] = rho - STEP * divergence
            for d in range(3):
                state[(1 + d) * ROWS : (2 + d) * ROWS] = field(flow, d) + STEP * (
                    -0.5 * grads[d] + 0.5 * field(laplace, d) + source[d * ROWS : (d + 1) * ROWS])
            state[4 * ROWS :] = field(flow, 3) + STEP * (
                -(2.0 / 3.0) * divergence + (2.0 / 3.0) * field(laplace, 3) + source[3 * ROWS :])
            return carry

        lax.fori_loop(0, MACRO_STEPS, sweep, 0)

    def coefficients(it):
        shift = target_ref[0, 0] - jnp.sum(mass[it]) / float(NX * NY * NZ * n_tx * n_ty)
        state[0:ROWS] = state[0:ROWS] + shift
        now = state[...]
        was = jnp.concatenate([gathered[it, SLOTS[c][0], :, SLOTS[c][1]].reshape(ROWS, CELLS) for c in range(5)], axis=0)
        change = now - was
        fluid = wall_rows[0]

        def own(value):
            return value.reshape(5, 2, ROWS // 2, CELLS)[:, 0, NX : 2 * NX]

        def put(at, value):
            coef[at * 5 * NX : (at + 1) * 5 * NX, :] = (value * fluid[None]).reshape(5 * NX, CELLS)

        here = own(change)
        put(0, 0.9 * here + STEP * own(now))
        for at, shift_of in enumerate((x_last, x_next, y_last, y_next, z_last, z_next)):
            put(1 + at, own(shift_of(change)) - here)
        for x in range(NX):
            c = coef[pl.ds(x, COEF, stride=NX), :]
            c_high = rounded(c)
            coef3[x] = jnp.concatenate([c_high, c - c_high, c_high, jnp.zeros((8, CELLS), f32)], axis=0).astype(bf16)

    def place(it, x, value):
        part[pl.ds(x, 16, stride=NX), :] = value

    for it in range(ITERS):
        if it == 0:
            for x in range(NX):
                loads[x].wait()
                place(0, x, projected(plane(0, x)))
            greeted = ring + 4 * len(near_tiles)

            @pl.when(my_set == MASS)
            def _():
                pl.semaphore_wait(barrier, greeted + len(only_far))

            @pl.when(my_set != MASS)
            def _():
                pl.semaphore_wait(barrier, greeted)

        for step in range(1, ring):
            rs_copy(it, step).start()

        def finalize(x, it=it):
            if it > 0:
                new = stream[x].reshape(CELLS, NV) + tn(coef3[x], rows3[...])
                h[it, x, 0:NY] = new.reshape(NY, NZ, NV)

        send_edges(it, finalize)
        if it == 0:
            prepare()

        rs[it, my_place] = part[pl.ds(pl.multiple_of(my_set * 4 * NX, 4 * NX), 4 * NX), :]
        for step in range(1, ring):
            rs_wait(it, step)
        total = rs[it, 0]
        for at in range(1, ring):
            total = total + rs[it, at]
        halves[it, 0] = total
        half_copy(it).start()
        send_more(it, PACE[0], PACE[1])
        stream_inside(it)
        half_copy(it).wait_recv()
        gathered[it, my_set, 1] = (total + halves[it, 1]).reshape(4, NX, CELLS)

        @pl.when(my_set == MASS)
        def _(it=it):
            for copy in tile_copies(it):
                copy.start()

        def send_all(depth, it=it):
            for copy in all_copies(it, depth):
                copy.start()

        for_depth(send_all)
        send_more(it, PACE[1], NX)

        if it == 0:
            prepare_rows()
        stream_ends(it)
        stream_sides(it, 0, EARLY)

        @pl.when(my_set == MASS)
        def _(it=it):
            total = gathered[it, my_set, 1, 3]
            for at, copy in enumerate(tile_copies(it)):
                copy.wait_recv()
                total = total + tile_mass[it, at]
            mass[it] = total
            for copy in mass_copies(it):
                copy.start()

        wait_all(it)
        macro_solve(it)
        stream_sides(it, EARLY, NX)

        @pl.when(my_set != MASS)
        def _(it=it):
            mass_copies(it)[0].wait_recv()

        coefficients(it)

        for step in range(1, ring):
            rs_copy(it, step).wait_send()
        if it + 1 < ITERS:
            for x in range(NX):
                at = pl.ds(x, 16, stride=NX)
                part[at, :] = stream_part[at, :] + jnp.dot(mixed3[...], coef3[x], preferred_element_type=f32)

    for x in range(NX):
        new = stream[x].reshape(CELLS, NV) + tn(coef3[x], rows3[...])
        dist_ref[x] = new.reshape(NY, NZ, NV)
    for k in range(5):
        value = state[k * ROWS + NX : k * ROWS + 2 * NX, :]
        for y in range(NY):
            moved = value if y == 0 else pltpu.roll(value, CELLS - y * NZ, 1)
            macro_ref[k, :, y, :] = moved[:, 0:NZ]

    for it in range(ITERS):
        half_copy(it).wait_send()
        for copy in x_copies(it):
            copy.wait_send()

        def sent(x, _, it=it):
            y_copy(it, x).wait_send()
            return 0

        lax.fori_loop(0, NX, sent, 0)

        def sent_all(depth, it=it):
            for copy in all_copies(it, depth):
                copy.wait_send()

        for_depth(sent_all)

        @pl.when(my_set == MASS)
        def _(it=it):
            for copy in tile_copies(it):
                copy.wait_send()
            for copy in mass_copies(it):
                copy.wait_send()


def on_device(sizes, initial, velocity, weights, wall, wall_temp, mass_target):
    n_tx, n_ty, n_vel = sizes
    dma = pltpu.SemaphoreType.DMA
    vmem = pl.BlockSpec(memory_space=pltpu.VMEM)
    tiles = n_tx * n_ty - 1
    return pl.pallas_call(
        functools.partial(kernel, sizes),
        out_shape=(jax.ShapeDtypeStruct((NX, NY, NZ, NV), f32), jax.ShapeDtypeStruct((5, NX, NY, NZ), f32)),
        in_specs=[pl.BlockSpec(memory_space=pltpu.HBM)] * 5 + [pl.BlockSpec(memory_space=pltpu.SMEM)],
        out_specs=(vmem, vmem),
        scratch_shapes=[
            pltpu.VMEM((ITERS, NX + 1, NY + 1, NZ, NV), f32),
            pltpu.VMEM((NX, NY, NZ, NV), f32),
            pltpu.VMEM((ITERS, NX, NZ, NV), f32),
            pltpu.VMEM((16 * NX, CELLS), f32),
            pltpu.VMEM((16 * NX, CELLS), f32),
            pltpu.VMEM((ITERS, n_vel // 2, 4 * NX, CELLS), f32),
            pltpu.VMEM((ITERS, 2, 4 * NX, CELLS), f32),
            pltpu.VMEM((ITERS, SETS, 6, 4, NX, CELLS), f32),
            pltpu.VMEM((ITERS, tiles, NX, CELLS), f32),
            pltpu.VMEM((ITERS, NX, CELLS), f32),
            pltpu.VMEM((COEF * NX, CELLS), f32),
            pltpu.VMEM((NX, 128, CELLS), bf16),
            pltpu.VMEM((128, NV), f32),
            pltpu.VMEM((128, NV), bf16),
            pltpu.VMEM((16, NV), f32),
            pltpu.VMEM((32, NV), bf16),
            pltpu.VMEM((16, 128), bf16),
            pltpu.VMEM((8, NV), f32),
            pltpu.VMEM((NX, CELLS, 128), f32),
            pltpu.VMEM((1, NX, CELLS), f32),
            pltpu.VMEM((5 * ROWS, CELLS), f32),
            pltpu.VMEM((4 * ROWS, CELLS), f32),
            pltpu.VMEM((3, NV), f32), pltpu.VMEM((NV,), f32),
            pltpu.VMEM((NX, NY, NZ), jnp.int32), pltpu.VMEM((NX, NY, NZ), f32),
            dma((NX,)), dma((4,)),
            dma((ITERS, n_vel // 2 - 1)), dma((ITERS, n_vel // 2)),
            dma((ITERS,)), dma((ITERS,)),
            dma((ITERS, 23)), dma((ITERS, SETS, 6)),
            dma((ITERS, tiles)), dma((ITERS, tiles)),
            dma((ITERS, 3)), dma((ITERS,)),
            dma((ITERS, NX + 2)), dma((ITERS, NX + 2)),
        ],
        compiler_params=pltpu.CompilerParams(collective_id=0, has_side_effects=True, vmem_limit_bytes=48 * 1024 * 1024),
    )(
        initial,
        *(pltpu.with_memory_space_constraint(a, pltpu.HBM) for a in (velocity, weights, wall, wall_temp)),
        mass_target.reshape(1, 1),
    )


def solution(mesh):
    sizes = (mesh.shape["tx"], mesh.shape["ty"], mesh.shape["vel"])
    placed = (
        P("tx", "ty", None, "vel"),
        P(None, "vel"),
        P("vel"),
        P("tx", "ty", None),
        P("tx", "ty", None),
        P(),
    )
    return jax.shard_map(
        functools.partial(on_device, sizes),
        mesh=mesh,
        in_specs=placed,
        out_specs=(P("tx", "ty", None, "vel"), P(None, "tx", "ty", None)),
        check_vma=False,
    )
```

```python
import functools

import jax
import jax.numpy as jnp
from jax import lax
from jax.experimental import pallas as pl
from jax.experimental.pallas import tpu as pltpu
from jax.sharding import PartitionSpec as P

ITERS = 3
MACRO_STEPS = 4
SETS = 4
DEPTH = (4, 3, 3, 3)
SLOTS = {0: (0, 0), 1: (0, 1), 2: (0, 2), 3: (0, 3), 4: (1, 0), 5: (1, 1), 6: (1, 2),
         8: (2, 0), 9: (2, 1), 10: (2, 2), 11: (3, 0), 12: (3, 1), 13: (3, 2)}
MASS = 3
STEP = 0.1
f32 = jnp.float32
bf16 = jnp.bfloat16
MESH = pl.DeviceIdType.MESH
NX, NY, NZ, NV = 8, 8, 16, 768
CELLS = NY * NZ
ROWS = 48
PACE = (4, 7)
EARLY = 6
REACH = 5
COEF = 40
FAR_FIRST = [(1, -1), (1, 1), (0, -1), (0, 1), (1, 0), (0, 0)]
NEIGHBOURS = [(0, -1), (0, 1), (1, -1), (1, 0), (1, 1)]


def rows_read(dx, dy):
    if dx == 0:
        return slice(0, NX)
    reach = REACH - dy
    return slice(NX - reach, NX) if dx == 1 else slice(0, reach)


def nt(a, b, precision=None):
    return lax.dot_general(a, b, (((1,), (1,)), ((), ())), precision=precision, preferred_element_type=f32)


def tn(a, b):
    return lax.dot_general(a, b, (((0,), (0,)), ((), ())), preferred_element_type=f32)


def rounded(value):
    return value.astype(bf16).astype(f32)


def lanes_of(value):
    return lax.broadcasted_iota(jnp.int32, value.shape, 1)


def other_half(value):
    parts = value.reshape(-1, 2, ROWS // 2, CELLS)
    return jnp.concatenate([parts[:, 1:2], parts[:, 0:1]], axis=1).reshape(value.shape)


def x_next(v):
    return pltpu.roll(v, v.shape[0] - 1, 0)


def x_last(v):
    return pltpu.roll(v, 1, 0)


def y_next(v):
    r = pltpu.roll(v, CELLS - NZ, 1)
    return jnp.where(lanes_of(v) < CELLS - NZ, r, other_half(r))


def y_last(v):
    r = pltpu.roll(v, NZ, 1)
    return jnp.where(lanes_of(v) >= NZ, r, other_half(r))


def z_next(v):
    return jnp.where((lanes_of(v) & (NZ - 1)) == NZ - 1, pltpu.roll(v, NZ - 1, 1), pltpu.roll(v, CELLS - 1, 1))


def z_last(v):
    return jnp.where((lanes_of(v) & (NZ - 1)) == 0, pltpu.roll(v, CELLS - NZ + 1, 1), pltpu.roll(v, 1, 1))


def field(v, k):
    return v[k * ROWS : (k + 1) * ROWS]


def kernel(
    sizes,
    init_ref, vel_in, weight_in, wall_in, wall_temp_in, target_ref,
    dist_ref, macro_ref,
    h, stream, edge_y, part, stream_part, rs, halves, gathered, tile_row, tile_mass, mass,
    coef, coef3, rows_f, rows3, proj_f, proj2, mixed3, factors, open_cells, wall_rows, state, source,
    velocity_ref, weight_ref, wall_ref, wall_temp_ref,
    load_sem, small_sem, rs_send, rs_recv, half_send, half_recv, all_send, all_recv,
    tile_send, tile_recv, mass_send, mass_recv, edge_send, edge_recv,
):
    n_tx, n_ty, n_vel = sizes
    tx, ty, me = lax.axis_index("tx"), lax.axis_index("ty"), lax.axis_index("vel")
    high_bit, low_bit = lax.rem(me // 4, 2), lax.rem(me, 2)
    my_set = high_bit * 2 + low_bit
    base = me - high_bit * 4 - low_bit

    def device(dx, dy, vel):
        return {"tx": lax.rem(tx + (dx + n_tx), n_tx), "ty": lax.rem(ty + dy, n_ty), "vel": vel}

    middle_bit = lax.rem(me // 2, 2)
    across = me + 2 - 4 * middle_bit
    ring = n_vel // 2
    my_place = me // 4 * 2 + low_bit

    def place_of(step):
        return lax.rem(my_place + step, ring)

    def group(step):
        at = place_of(step)
        return at // 2 * 4 + middle_bit * 2 + lax.rem(at, 2)

    def set_of(vel):
        return lax.rem(vel // 4, 2) * 2 + lax.rem(vel, 2)

    def mate(a, b):
        return base + lax.rem(high_bit + a, 2) * 4 + lax.rem(low_bit + b, 2)

    mates = [(0, 1), (1, 0), (1, 1)]
    far_tiles = [(a, b) for b in range(n_ty) for a in range(n_tx) if (a, b) != (0, 0)]
    near_tiles = [(dx % n_tx, dy) for dy, dx in NEIGHBOURS]
    only_far = [t for t in far_tiles if t not in near_tiles]

    loads = [pltpu.make_async_copy(init_ref.at[x], h.at[0, x, 0:NY], load_sem.at[x]) for x in range(NX)]
    smalls = [pltpu.make_async_copy(a, b, small_sem.at[at]) for at, (a, b) in enumerate(
        ((vel_in, velocity_ref), (weight_in, weight_ref), (wall_in, wall_ref), (wall_temp_in, wall_temp_ref)))]
    for copy in smalls + loads:
        copy.start()

    barrier = pltpu.get_barrier_semaphore()
    for step in range(1, ring):
        pl.semaphore_signal(barrier, inc=1, device_id=device(0, 0, group(step)), device_id_type=MESH)
    pl.semaphore_signal(barrier, inc=1, device_id=device(0, 0, across), device_id_type=MESH)
    for a, b in [(0, 0)] + mates:
        for dx, dy in near_tiles:
            pl.semaphore_signal(barrier, inc=1, device_id=device(dx, dy, mate(a, b)), device_id_type=MESH)

    @pl.when(my_set == MASS)
    def _():
        for a, b in only_far:
            pl.semaphore_signal(barrier, inc=1, device_id=device(a, b, me), device_id_type=MESH)

    smalls[0].wait()
    smalls[1].wait()
    vx, vy, vz = velocity_ref[0:1, :], velocity_ref[1:2, :], velocity_ref[2:3, :]
    speed_sq = vx * vx + vy * vy + vz * vz
    ones = jnp.ones_like(vx)
    basis = [ones, 2.0 * vx, 2.0 * vy, 2.0 * vz, speed_sq - 1.5]
    sides = []
    for v in (vx, vy, vz):
        sides += [STEP * jnp.maximum(v, 0.0), -STEP * jnp.minimum(v, 0.0)]
    scale = weight_ref[...].reshape(1, NV) / float(NV * n_vel)
    none = jnp.zeros_like(vx)
    moments = [ones, vx, vy, vz,
               (2.0 / 3.0) * speed_sq - 1.0, 2.0 * (vx * vx - speed_sq / 3.0), 2.0 * (vy * vy - speed_sq / 3.0), none,
               2.0 * vx * vy, 2.0 * vx * vz, 2.0 * vy * vz, none,
               vx * (speed_sq - 2.5), vy * (speed_sq - 2.5), vz * (speed_sq - 2.5), ones]
    for at, row in enumerate(moments):
        proj_f[at : at + 1, :] = row * scale
    proj = proj_f[...]
    proj2[...] = jnp.concatenate([rounded(proj), proj - rounded(proj)], axis=0).astype(bf16)

    def prepare():
        bx, by, bz = (STEP * jnp.abs(v) for v in (vx, vy, vz))
        for at, row in enumerate((0.9 - bx - by - bz, bx, by, bz, vz)):
            factors[at : at + 1, :] = row
        smalls[2].wait()
        smalls[3].wait()
        solid = jnp.zeros((NX, CELLS), f32)
        heat = jnp.zeros((NX, CELLS), f32)
        for y in range(NY):
            spread = (lax.broadcasted_iota(jnp.int32, (NZ, CELLS), 1)
                      == lax.broadcasted_iota(jnp.int32, (NZ, CELLS), 0) + y * NZ).astype(f32)
            is_wall = (wall_ref[:, y, :] == 1).astype(f32)
            both = jnp.concatenate([is_wall, is_wall * wall_temp_ref[:, y, :]], axis=0)
            moved = lax.dot_general(both, spread, (((1,), (0,)), ((), ())), precision=lax.Precision.HIGHEST,
                                    preferred_element_type=f32)
            solid = solid + moved[0:NX]
            heat = heat + moved[NX:]
        fluid = 1.0 - solid
        wall_rows[0] = fluid
        for x in range(NX):
            open_cells[x] = jnp.broadcast_to(fluid[x : x + 1], (CELLS, CELLS)).T
        coef[35 * NX : 36 * NX, :] = heat
        coef[36 * NX :, :] = jnp.zeros((4 * NX, CELLS), f32)

    def prepare_rows():
        rows = basis + [side * b for side in sides for b in basis] + [basis[4]]
        for copy in range(3):
            for at, row in enumerate(rows):
                rows_f[copy * COEF + at : copy * COEF + at + 1, :] = row
            rows_f[copy * COEF + len(rows) : (copy + 1) * COEF, :] = jnp.zeros((COEF - len(rows), NV), f32)
        rows_f[3 * COEF :, :] = jnp.zeros((128 - 3 * COEF, NV), f32)
        every = rows_f[...]
        high = rounded(every)
        rows3[...] = jnp.where(lax.broadcasted_iota(jnp.int32, every.shape, 0) < 2 * COEF, high, every - high).astype(bf16)
        mixed = nt(proj_f[...], every, lax.Precision.HIGHEST)
        mixed_high = rounded(mixed)
        mixed3[...] = jnp.where(lanes_of(mixed) < 2 * COEF, mixed_high, mixed - mixed_high).astype(bf16)

    def projected(value):
        top = value.astype(bf16)
        low = (value - top.astype(f32)).astype(bf16)
        both = nt(proj2[...], top)
        return both[0:16] + both[16:32] + nt(proj2[0:16, :], low)

    def plane(it, x):
        return h[it, x, 0:NY].reshape(CELLS, NV)

    def pack_edge(it, x):
        top, bottom = h[it, x, NY - 1], h[it, x, 0]
        for t in range(6):
            cut = slice(t * 128, (t + 1) * 128)
            if t in (0, 3):
                piece = top[:, cut]
            elif t in (2, 5):
                piece = bottom[:, cut]
            else:
                piece = jnp.where(lanes_of(top[:, cut]) < 64, top[:, cut], bottom[:, cut])
            edge_y[it, x, :, cut] = piece

    def ordered(at):
        return lax.rem(at * (NX - 1), NX)

    def y_copy(it, x):
        return pltpu.make_async_remote_copy(
            src_ref=edge_y.at[it, x], dst_ref=h.at[it, x, NY],
            send_sem=edge_send.at[it, x], recv_sem=edge_recv.at[it, x],
            device_id=device(0, 1, me), device_id_type=MESH)

    def x_copies(it):
        half = NV // 2
        return [
            pltpu.make_async_remote_copy(
                src_ref=h.at[it, 0, 0:NY, :, half:NV], dst_ref=h.at[it, NX, 0:NY, :, half:NV],
                send_sem=edge_send.at[it, NX], recv_sem=edge_recv.at[it, NX],
                device_id=device(-1, 0, me), device_id_type=MESH),
            pltpu.make_async_remote_copy(
                src_ref=h.at[it, NX - 1, 0:NY, :, 0:half], dst_ref=h.at[it, NX, 0:NY, :, 0:half],
                send_sem=edge_send.at[it, NX + 1], recv_sem=edge_recv.at[it, NX + 1],
                device_id=device(1, 0, me), device_id_type=MESH),
        ]

    def send_edges(it, fill):
        def body(at, _):
            x = ordered(at)
            fill(x)
            pack_edge(it, x)
            pl.when(at < PACE[0])(y_copy(it, x).start)
            return 0

        lax.fori_loop(0, 2, body, 0)
        for copy in x_copies(it):
            copy.start()
        lax.fori_loop(2, NX, body, 0)

    def send_more(it, first, last):
        def body(at, _):
            y_copy(it, ordered(at)).start()
            return 0

        lax.fori_loop(first, last, body, 0)

    def stream_cell(it, x, y):
        half = NV // 2
        x_down, x_up = lax.rem(x + NX, NX + 1), x + 1
        y_down, y_up = (y + NY) % (NY + 1), y + 1
        for t in range(6):
            cut = slice(t * 128, (t + 1) * 128)
            own = h[it, x, y, :, cut]
            from_x = h[it, x_down if t < 3 else x_up, y, :, cut]
            if t in (0, 3):
                from_y = h[it, x, y_down, :, cut]
            elif t in (2, 5):
                from_y = h[it, x, y_up, :, cut]
            else:
                from_y = jnp.where(lanes_of(own) < 64, h[it, x, y_down, :, cut], h[it, x, y_up, :, cut])
            up = jnp.broadcast_to(factors[4:5, cut], own.shape) > 0.0
            from_z = jnp.where(up, pltpu.roll(own, 1, 0), pltpu.roll(own, NZ - 1, 0))
            value = (factors[0:1, cut] * own + factors[1:2, cut] * from_x
                     + factors[2:3, cut] * from_y + factors[3:4, cut] * from_z)
            stream[x, y, :, cut] = value * open_cells[x, y * NZ : (y + 1) * NZ, :]

    def stream_inside(it):
        def body(x, _):
            for y in range(1, NY - 1):
                stream_cell(it, x, y)
            return 0

        lax.fori_loop(1, NX - 1, body, 0)

    def stream_ends(it):
        for copy in x_copies(it):
            copy.wait_recv()

        def body(side, _):
            for y in range(1, NY - 1):
                stream_cell(it, side * (NX - 1), y)
            return 0

        lax.fori_loop(0, 2, body, 0)

    def stream_sides(it, first, last):
        def body(at, _):
            x = ordered(at)
            y_copy(it, x).wait_recv()
            stream_cell(it, x, 0)
            stream_cell(it, x, NY - 1)
            if it + 1 < ITERS:
                stream_part[pl.ds(x, 16, stride=NX), :] = projected(stream[x].reshape(CELLS, NV))
            return 0

        lax.fori_loop(first, last, body, 0)

    def rs_copy(it, step):
        target = group(step)
        return pltpu.make_async_remote_copy(
            src_ref=part.at[pl.ds(pl.multiple_of(set_of(target) * 4 * NX, 4 * NX), 4 * NX)], dst_ref=rs.at[it, my_place],
            send_sem=rs_send.at[it, step - 1], recv_sem=rs_recv.at[it, my_place],
            device_id=device(0, 0, target), device_id_type=MESH)

    def rs_wait(it, step):
        at = place_of(step)
        pltpu.make_async_remote_copy(
            src_ref=part.at[0 : 4 * NX], dst_ref=rs.at[it, at],
            send_sem=rs_send.at[it, step - 1], recv_sem=rs_recv.at[it, at],
            device_id=device(0, 0, group(step)), device_id_type=MESH).wait_recv()

    def half_copy(it):
        return pltpu.make_async_remote_copy(
            src_ref=halves.at[it, 0], dst_ref=halves.at[it, 1],
            send_sem=half_send.at[it], recv_sem=half_recv.at[it],
            device_id=device(0, 0, across), device_id_type=MESH)

    def all_copies(it, depth):
        copies = []
        for dy, dx in FAR_FIRST:
            for a, b in mates[::-1] + [(0, 0)]:
                if (a, b, dx, dy) == (0, 0, 0, 0):
                    continue
                slot = dy * 3 + 1 - dx
                cut = rows_read(dx, dy)
                copies.append(pltpu.make_async_remote_copy(
                    src_ref=gathered.at[it, my_set, 1, 0:depth, cut], dst_ref=gathered.at[it, my_set, slot, 0:depth, cut],
                    send_sem=all_send.at[it, len(copies)], recv_sem=all_recv.at[it, my_set, slot],
                    device_id=device(dx, dy, mate(a, b)), device_id_type=MESH))
        return copies

    def for_depth(action):
        for depth in sorted(set(DEPTH)):
            wanted = [at for at in range(SETS) if DEPTH[at] == depth]
            match = my_set == wanted[0]
            for at in wanted[1:]:
                match = jnp.logical_or(match, my_set == at)

            @pl.when(match)
            def _(depth=depth):
                action(depth)

    def wait_all(it):
        for at in range(SETS):
            for slot in range(6):
                dx = 1 - slot % 3
                cut = rows_read(dx, slot // 3)

                def wait(at=at, slot=slot, cut=cut):
                    pltpu.make_async_remote_copy(
                        src_ref=gathered.at[it, at, 1, 0 : DEPTH[at], cut],
                        dst_ref=gathered.at[it, at, slot, 0 : DEPTH[at], cut],
                        send_sem=all_send.at[it, 0], recv_sem=all_recv.at[it, at, slot],
                        device_id=device(0, 0, group(1)), device_id_type=MESH).wait_recv()

                if slot == 1:
                    pl.when(my_set != at)(wait)
                else:
                    wait()

    def tile_copies(it):
        return [
            pltpu.make_async_remote_copy(
                src_ref=tile_row.at[it], dst_ref=tile_mass.at[it, at],
                send_sem=tile_send.at[it, at], recv_sem=tile_recv.at[it, at],
                device_id=device(a, b, me), device_id_type=MESH)
            for at, (a, b) in enumerate(far_tiles)
        ]

    def mass_copies(it):
        return [
            pltpu.make_async_remote_copy(
                src_ref=mass.at[it], dst_ref=mass.at[it],
                send_sem=mass_send.at[it, at], recv_sem=mass_recv.at[it],
                device_id=device(0, 0, mate(a, b)), device_id_type=MESH)
            for at, (a, b) in enumerate(mates)
        ]

    def macro_solve(it):
        def g(c):
            if c == 7:
                return -(g(5) + g(6))
            at, k = SLOTS[c]
            return gathered[it, at, :, k].reshape(ROWS, CELLS)

        def many(*cs):
            return jnp.concatenate([g(c) for c in cs], axis=0)

        flow = many(1, 2, 3, 4)
        along = (many(5, 8, 9, 11), many(8, 6, 10, 12), many(9, 10, 7, 13))
        shifts = ((x_next, x_last), (y_next, y_last), (z_next, z_last))
        total = -6.0 * flow
        for (after, before), a in zip(shifts, along):
            total = total + (after(flow + 0.5 * a) + before(flow - 0.5 * a))
        source[0 : 3 * ROWS] = -0.5 * total[0 : 3 * ROWS]
        source[3 * ROWS :] = -(2.0 / 3.0) * total[3 * ROWS :]
        state[...] = many(0, 1, 2, 3, 4)

        def sweep(_, carry):
            rho, flow = state[0:ROWS], state[ROWS : 5 * ROWS]
            stack = jnp.concatenate([rho + field(flow, 3), flow], axis=0)
            laplace = -6.0 * flow
            grads, divergence = [], None
            for d, (after, before) in enumerate(shifts):
                up, down = after(stack), before(stack)
                laplace = laplace + (up[ROWS:] + down[ROWS:])
                grads.append(0.5 * (field(up, 0) - field(down, 0)))
                part_div = 0.5 * (field(up, 1 + d) - field(down, 1 + d))
                divergence = part_div if divergence is None else divergence + part_div
            state[0:ROWS] = rho - STEP * divergence
            for d in range(3):
                state[(1 + d) * ROWS : (2 + d) * ROWS] = field(flow, d) + STEP * (
                    -0.5 * grads[d] + 0.5 * field(laplace, d) + source[d * ROWS : (d + 1) * ROWS])
            state[4 * ROWS :] = field(flow, 3) + STEP * (
                -(2.0 / 3.0) * divergence + (2.0 / 3.0) * field(laplace, 3) + source[3 * ROWS :])
            return carry

        lax.fori_loop(0, MACRO_STEPS, sweep, 0)

    def coefficients(it):
        shift = target_ref[0, 0] - jnp.sum(mass[it]) / float(NX * NY * NZ * n_tx * n_ty)
        state[0:ROWS] = state[0:ROWS] + shift
        now = state[...]
        was = jnp.concatenate([gathered[it, SLOTS[c][0], :, SLOTS[c][1]].reshape(ROWS, CELLS) for c in range(5)], axis=0)
        change = now - was
        fluid = wall_rows[0]

        def tile(value, half):
            return value.reshape(5, 2, ROWS // 2, CELLS)[:, half, NX : 2 * NX].reshape(5 * NX, CELLS)

        def along_x(value):
            return value.reshape(5, ROWS // 2, CELLS)[:, NX : 2 * NX].reshape(5 * NX, CELLS)

        def put(at, value):
            coef[at * 5 * NX : (at + 1) * 5 * NX, :] = (value.reshape(5, NX, CELLS) * fluid[None]).reshape(5 * NX, CELLS)

        here, other = tile(change, 0), tile(change, 1)
        strip = change.reshape(5, 2, ROWS // 2, CELLS)[:, 0].reshape(5 * ROWS // 2, CELLS)
        lane = lanes_of(here)
        put(0, 0.9 * here + STEP * tile(now, 0))
        put(1, along_x(x_last(strip)) - here)
        put(2, along_x(x_next(strip)) - here)
        put(3, jnp.where(lane >= NZ, pltpu.roll(here, NZ, 1), pltpu.roll(other, NZ, 1)) - here)
        put(4, jnp.where(lane < CELLS - NZ, pltpu.roll(here, CELLS - NZ, 1), pltpu.roll(other, CELLS - NZ, 1)) - here)
        put(5, z_last(here) - here)
        put(6, z_next(here) - here)
        for x in range(NX):
            c = coef[pl.ds(x, COEF, stride=NX), :]
            c_high = rounded(c)
            coef3[x] = jnp.concatenate([c_high, c - c_high, c_high, jnp.zeros((8, CELLS), f32)], axis=0).astype(bf16)

    def place(it, x, value):
        part[pl.ds(x, 16, stride=NX), :] = value

    for it in range(ITERS):
        if it == 0:
            for x in range(NX):
                loads[x].wait()
                place(0, x, projected(plane(0, x)))
            greeted = ring + 4 * len(near_tiles)

            @pl.when(my_set == MASS)
            def _():
                pl.semaphore_wait(barrier, greeted + len(only_far))

            @pl.when(my_set != MASS)
            def _():
                pl.semaphore_wait(barrier, greeted)

        for step in range(1, ring):
            rs_copy(it, step).start()

        def finalize(x, it=it):
            if it > 0:
                new = stream[x].reshape(CELLS, NV) + tn(coef3[x], rows3[...])
                h[it, x, 0:NY] = new.reshape(NY, NZ, NV)

        send_edges(it, finalize)
        if it == 0:
            prepare()

        rs[it, my_place] = part[pl.ds(pl.multiple_of(my_set * 4 * NX, 4 * NX), 4 * NX), :]
        for step in range(1, ring):
            rs_wait(it, step)
        total = rs[it, 0]
        for at in range(1, ring):
            total = total + rs[it, at]
        halves[it, 0] = total
        half_copy(it).start()
        send_more(it, PACE[0], PACE[1])
        stream_inside(it)
        half_copy(it).wait_recv()
        gathered[it, my_set, 1] = (total + halves[it, 1]).reshape(4, NX, CELLS)

        def send_all(depth, it=it):
            for copy in all_copies(it, depth):
                copy.start()

        for_depth(send_all)

        @pl.when(my_set == MASS)
        def _(it=it):
            tile_row[it] = jnp.sum(gathered[it, my_set, 1, 3], axis=0, keepdims=True)
            for copy in tile_copies(it):
                copy.start()

        send_more(it, PACE[1], NX)

        if it == 0:
            prepare_rows()
        stream_ends(it)
        stream_sides(it, 0, EARLY)

        @pl.when(my_set == MASS)
        def _(it=it):
            total = tile_row[it]
            for at, copy in enumerate(tile_copies(it)):
                copy.wait_recv()
                total = total + tile_mass[it, at]
            mass[it] = total
            for copy in mass_copies(it):
                copy.start()

        wait_all(it)
        macro_solve(it)
        stream_sides(it, EARLY, NX)

        @pl.when(my_set != MASS)
        def _(it=it):
            mass_copies(it)[0].wait_recv()

        coefficients(it)

        for step in range(1, ring):
            rs_copy(it, step).wait_send()
        if it + 1 < ITERS:
            for x in range(NX):
                at = pl.ds(x, 16, stride=NX)
                part[at, :] = stream_part[at, :] + jnp.dot(mixed3[...], coef3[x], preferred_element_type=f32)

    for x in range(NX):
        new = stream[x].reshape(CELLS, NV) + tn(coef3[x], rows3[...])
        dist_ref[x] = new.reshape(NY, NZ, NV)
    for k in range(5):
        value = state[k * ROWS + NX : k * ROWS + 2 * NX, :]
        for y in range(NY):
            moved = value if y == 0 else pltpu.roll(value, CELLS - y * NZ, 1)
            macro_ref[k, :, y, :] = moved[:, 0:NZ]

    for it in range(ITERS):
        half_copy(it).wait_send()
        for copy in x_copies(it):
            copy.wait_send()

        def sent(x, _, it=it):
            y_copy(it, x).wait_send()
            return 0

        lax.fori_loop(0, NX, sent, 0)

        def sent_all(depth, it=it):
            for copy in all_copies(it, depth):
                copy.wait_send()

        for_depth(sent_all)

        @pl.when(my_set == MASS)
        def _(it=it):
            for copy in tile_copies(it):
                copy.wait_send()
            for copy in mass_copies(it):
                copy.wait_send()


def on_device(sizes, initial, velocity, weights, wall, wall_temp, mass_target):
    n_tx, n_ty, n_vel = sizes
    dma = pltpu.SemaphoreType.DMA
    vmem = pl.BlockSpec(memory_space=pltpu.VMEM)
    tiles = n_tx * n_ty - 1
    return pl.pallas_call(
        functools.partial(kernel, sizes),
        out_shape=(jax.ShapeDtypeStruct((NX, NY, NZ, NV), f32), jax.ShapeDtypeStruct((5, NX, NY, NZ), f32)),
        in_specs=[pl.BlockSpec(memory_space=pltpu.HBM)] * 5 + [pl.BlockSpec(memory_space=pltpu.SMEM)],
        out_specs=(vmem, vmem),
        scratch_shapes=[
            pltpu.VMEM((ITERS, NX + 1, NY + 1, NZ, NV), f32),
            pltpu.VMEM((NX, NY, NZ, NV), f32),
            pltpu.VMEM((ITERS, NX, NZ, NV), f32),
            pltpu.VMEM((16 * NX, CELLS), f32),
            pltpu.VMEM((16 * NX, CELLS), f32),
            pltpu.VMEM((ITERS, n_vel // 2, 4 * NX, CELLS), f32),
            pltpu.VMEM((ITERS, 2, 4 * NX, CELLS), f32),
            pltpu.VMEM((ITERS, SETS, 6, 4, NX, CELLS), f32),
            pltpu.VMEM((ITERS, 1, CELLS), f32),
            pltpu.VMEM((ITERS, tiles, 1, CELLS), f32),
            pltpu.VMEM((ITERS, 1, CELLS), f32),
            pltpu.VMEM((COEF * NX, CELLS), f32),
            pltpu.VMEM((NX, 128, CELLS), bf16),
            pltpu.VMEM((128, NV), f32),
            pltpu.VMEM((128, NV), bf16),
            pltpu.VMEM((16, NV), f32),
            pltpu.VMEM((32, NV), bf16),
            pltpu.VMEM((16, 128), bf16),
            pltpu.VMEM((8, NV), f32),
            pltpu.VMEM((NX, CELLS, 128), f32),
            pltpu.VMEM((1, NX, CELLS), f32),
            pltpu.VMEM((5 * ROWS, CELLS), f32),
            pltpu.VMEM((4 * ROWS, CELLS), f32),
            pltpu.VMEM((3, NV), f32), pltpu.VMEM((NV,), f32),
            pltpu.VMEM((NX, NY, NZ), jnp.int32), pltpu.VMEM((NX, NY, NZ), f32),
            dma((NX,)), dma((4,)),
            dma((ITERS, n_vel // 2 - 1)), dma((ITERS, n_vel // 2)),
            dma((ITERS,)), dma((ITERS,)),
            dma((ITERS, 23)), dma((ITERS, SETS, 6)),
            dma((ITERS, tiles)), dma((ITERS, tiles)),
            dma((ITERS, 3)), dma((ITERS,)),
            dma((ITERS, NX + 2)), dma((ITERS, NX + 2)),
        ],
        compiler_params=pltpu.CompilerParams(collective_id=0, has_side_effects=True, vmem_limit_bytes=48 * 1024 * 1024),
    )(
        initial,
        *(pltpu.with_memory_space_constraint(a, pltpu.HBM) for a in (velocity, weights, wall, wall_temp)),
        mass_target.reshape(1, 1),
    )


def solution(mesh):
    sizes = (mesh.shape["tx"], mesh.shape["ty"], mesh.shape["vel"])
    placed = (
        P("tx", "ty", None, "vel"),
        P(None, "vel"),
        P("vel"),
        P("tx", "ty", None),
        P("tx", "ty", None),
        P(),
    )
    return jax.shard_map(
        functools.partial(on_device, sizes),
        mesh=mesh,
        in_specs=placed,
        out_specs=(P("tx", "ty", None, "vel"), P(None, "tx", "ty", None)),
        check_vma=False,
    )
```

```python
import functools

import jax
import jax.numpy as jnp
from jax import lax
from jax.experimental import pallas as pl
from jax.experimental.pallas import tpu as pltpu
from jax.sharding import PartitionSpec as P

ITERS = 3
MACRO_STEPS = 4
SETS = 4
DEPTH = (4, 3, 3, 3)
SLOTS = {0: (0, 0), 1: (0, 1), 2: (0, 2), 3: (0, 3), 4: (1, 0), 5: (1, 1), 6: (1, 2),
         8: (2, 0), 9: (2, 1), 10: (2, 2), 11: (3, 0), 12: (3, 1), 13: (3, 2)}
MASS = 3
STEP = 0.1
f32 = jnp.float32
bf16 = jnp.bfloat16
MESH = pl.DeviceIdType.MESH
NX, NY, NZ, NV = 8, 8, 16, 768
CELLS = NY * NZ
ROWS = 48
PACE = (4, 7)
EARLY = 6
REACH = 5
COEF = 40
FAR_FIRST = [(1, -1), (1, 1), (0, -1), (0, 1), (1, 0), (0, 0)]
NEIGHBOURS = [(0, -1), (0, 1), (1, -1), (1, 0), (1, 1)]


def rows_read(dx, dy):
    if dx == 0:
        return slice(0, NX)
    reach = REACH - dy
    return slice(NX - reach, NX) if dx == 1 else slice(0, reach)


def nt(a, b, precision=None):
    return lax.dot_general(a, b, (((1,), (1,)), ((), ())), precision=precision, preferred_element_type=f32)


def tn(a, b):
    return lax.dot_general(a, b, (((0,), (0,)), ((), ())), preferred_element_type=f32)


def rounded(value):
    return value.astype(bf16).astype(f32)


def lanes_of(value):
    return lax.broadcasted_iota(jnp.int32, value.shape, 1)


def other_half(value):
    parts = value.reshape(-1, 2, ROWS // 2, CELLS)
    return jnp.concatenate([parts[:, 1:2], parts[:, 0:1]], axis=1).reshape(value.shape)


def x_next(v):
    return pltpu.roll(v, v.shape[0] - 1, 0)


def x_last(v):
    return pltpu.roll(v, 1, 0)


def y_next(v):
    r = pltpu.roll(v, CELLS - NZ, 1)
    return jnp.where(lanes_of(v) < CELLS - NZ, r, other_half(r))


def y_last(v):
    r = pltpu.roll(v, NZ, 1)
    return jnp.where(lanes_of(v) >= NZ, r, other_half(r))


def z_next(v):
    return jnp.where((lanes_of(v) & (NZ - 1)) == NZ - 1, pltpu.roll(v, NZ - 1, 1), pltpu.roll(v, CELLS - 1, 1))


def z_last(v):
    return jnp.where((lanes_of(v) & (NZ - 1)) == 0, pltpu.roll(v, CELLS - NZ + 1, 1), pltpu.roll(v, 1, 1))


def field(v, k):
    return v[k * ROWS : (k + 1) * ROWS]


def kernel(
    sizes,
    init_ref, vel_in, weight_in, wall_in, wall_temp_in, target_ref,
    dist_ref, macro_ref,
    h, stream, edge_y, part, stream_part, rs, halves, gathered, tile_row, tile_mass, mass,
    coef, coef3, rows_f, rows3, proj_f, proj2, mixed3, factors, open_cells, wall_rows, state, source,
    velocity_ref, weight_ref, wall_ref, wall_temp_ref,
    load_sem, small_sem, rs_send, rs_recv, half_send, half_recv, all_send, all_recv,
    tile_send, tile_recv, mass_send, mass_recv, edge_send, edge_recv,
):
    n_tx, n_ty, n_vel = sizes
    tx, ty, me = lax.axis_index("tx"), lax.axis_index("ty"), lax.axis_index("vel")
    high_bit, low_bit = lax.rem(me // 4, 2), lax.rem(me, 2)
    my_set = high_bit * 2 + low_bit
    base = me - high_bit * 4 - low_bit

    def device(dx, dy, vel):
        return {"tx": lax.rem(tx + (dx + n_tx), n_tx), "ty": lax.rem(ty + dy, n_ty), "vel": vel}

    middle_bit = lax.rem(me // 2, 2)
    across = me + 2 - 4 * middle_bit
    ring = n_vel // 2
    my_place = me // 4 * 2 + low_bit

    def place_of(step):
        return lax.rem(my_place + step, ring)

    def group(step):
        at = place_of(step)
        return at // 2 * 4 + middle_bit * 2 + lax.rem(at, 2)

    def set_of(vel):
        return lax.rem(vel // 4, 2) * 2 + lax.rem(vel, 2)

    def mate(a, b):
        return base + lax.rem(high_bit + a, 2) * 4 + lax.rem(low_bit + b, 2)

    mates = [(0, 1), (1, 0), (1, 1)]
    far_tiles = [(a, b) for b in range(n_ty) for a in range(n_tx) if (a, b) != (0, 0)]
    near_tiles = [(dx % n_tx, dy) for dy, dx in NEIGHBOURS]
    only_far = [t for t in far_tiles if t not in near_tiles]

    loads = [pltpu.make_async_copy(init_ref.at[x], h.at[0, x, 0:NY], load_sem.at[x]) for x in range(NX)]
    smalls = [pltpu.make_async_copy(a, b, small_sem.at[at]) for at, (a, b) in enumerate(
        ((vel_in, velocity_ref), (weight_in, weight_ref), (wall_in, wall_ref), (wall_temp_in, wall_temp_ref)))]
    for copy in smalls + loads:
        copy.start()

    barrier = pltpu.get_barrier_semaphore()
    for step in range(1, ring):
        pl.semaphore_signal(barrier, inc=1, device_id=device(0, 0, group(step)), device_id_type=MESH)
    pl.semaphore_signal(barrier, inc=1, device_id=device(0, 0, across), device_id_type=MESH)
    for a, b in [(0, 0)] + mates:
        for dx, dy in near_tiles:
            pl.semaphore_signal(barrier, inc=1, device_id=device(dx, dy, mate(a, b)), device_id_type=MESH)

    @pl.when(my_set == MASS)
    def _():
        for a, b in only_far:
            pl.semaphore_signal(barrier, inc=1, device_id=device(a, b, me), device_id_type=MESH)

    smalls[0].wait()
    smalls[1].wait()
    vx, vy, vz = velocity_ref[0:1, :], velocity_ref[1:2, :], velocity_ref[2:3, :]
    speed_sq = vx * vx + vy * vy + vz * vz
    ones = jnp.ones_like(vx)
    basis = [ones, 2.0 * vx, 2.0 * vy, 2.0 * vz, speed_sq - 1.5]
    sides = []
    for v in (vx, vy, vz):
        sides += [STEP * jnp.maximum(v, 0.0), -STEP * jnp.minimum(v, 0.0)]
    scale = weight_ref[...].reshape(1, NV) / float(NV * n_vel)
    none = jnp.zeros_like(vx)
    moments = [ones, vx, vy, vz,
               (2.0 / 3.0) * speed_sq - 1.0, 2.0 * (vx * vx - speed_sq / 3.0), 2.0 * (vy * vy - speed_sq / 3.0), none,
               2.0 * vx * vy, 2.0 * vx * vz, 2.0 * vy * vz, none,
               vx * (speed_sq - 2.5), vy * (speed_sq - 2.5), vz * (speed_sq - 2.5), ones]
    for at, row in enumerate(moments):
        proj_f[at : at + 1, :] = row * scale
    proj = proj_f[...]
    proj2[...] = jnp.concatenate([rounded(proj), proj - rounded(proj)], axis=0).astype(bf16)

    def prepare():
        bx, by, bz = (STEP * jnp.abs(v) for v in (vx, vy, vz))
        for at, row in enumerate((0.9 - bx - by - bz, bx, by, bz, vz)):
            factors[at : at + 1, :] = row
        smalls[2].wait()
        smalls[3].wait()
        solid = jnp.zeros((NX, CELLS), f32)
        heat = jnp.zeros((NX, CELLS), f32)
        for y in range(NY):
            spread = (lax.broadcasted_iota(jnp.int32, (NZ, CELLS), 1)
                      == lax.broadcasted_iota(jnp.int32, (NZ, CELLS), 0) + y * NZ).astype(f32)
            is_wall = (wall_ref[:, y, :] == 1).astype(f32)
            both = jnp.concatenate([is_wall, is_wall * wall_temp_ref[:, y, :]], axis=0)
            moved = lax.dot_general(both, spread, (((1,), (0,)), ((), ())), precision=lax.Precision.HIGHEST,
                                    preferred_element_type=f32)
            solid = solid + moved[0:NX]
            heat = heat + moved[NX:]
        fluid = 1.0 - solid
        wall_rows[0] = fluid
        for x in range(NX):
            open_cells[x] = jnp.broadcast_to(fluid[x : x + 1], (CELLS, CELLS)).T
        coef[35 * NX : 36 * NX, :] = heat
        coef[36 * NX :, :] = jnp.zeros((4 * NX, CELLS), f32)

    def prepare_rows():
        rows = basis + [side * b for side in sides for b in basis] + [basis[4]]
        for copy in range(3):
            for at, row in enumerate(rows):
                rows_f[copy * COEF + at : copy * COEF + at + 1, :] = row
            rows_f[copy * COEF + len(rows) : (copy + 1) * COEF, :] = jnp.zeros((COEF - len(rows), NV), f32)
        rows_f[3 * COEF :, :] = jnp.zeros((128 - 3 * COEF, NV), f32)
        every = rows_f[...]
        high = rounded(every)
        rows3[...] = jnp.where(lax.broadcasted_iota(jnp.int32, every.shape, 0) < 2 * COEF, high, every - high).astype(bf16)
        mixed = nt(proj_f[...], every, lax.Precision.HIGHEST)
        mixed_high = rounded(mixed)
        mixed3[...] = jnp.where(lanes_of(mixed) < 2 * COEF, mixed_high, mixed - mixed_high).astype(bf16)

    def projected(value):
        top = value.astype(bf16)
        low = (value - top.astype(f32)).astype(bf16)
        both = nt(proj2[...], top)
        return both[0:16] + both[16:32] + nt(proj2[0:16, :], low)

    def plane(it, x):
        return h[it, x, 0:NY].reshape(CELLS, NV)

    def pack_edge(it, x):
        top, bottom = h[it, x, NY - 1], h[it, x, 0]
        for t in range(6):
            cut = slice(t * 128, (t + 1) * 128)
            if t in (0, 3):
                piece = top[:, cut]
            elif t in (2, 5):
                piece = bottom[:, cut]
            else:
                piece = jnp.where(lanes_of(top[:, cut]) < 64, top[:, cut], bottom[:, cut])
            edge_y[it, x, :, cut] = piece

    def ordered(at):
        return lax.rem(at * (NX - 1), NX)

    def y_copy(it, x):
        return pltpu.make_async_remote_copy(
            src_ref=edge_y.at[it, x], dst_ref=h.at[it, x, NY],
            send_sem=edge_send.at[it, x], recv_sem=edge_recv.at[it, x],
            device_id=device(0, 1, me), device_id_type=MESH)

    def x_copies(it):
        half = NV // 2
        return [
            pltpu.make_async_remote_copy(
                src_ref=h.at[it, 0, 0:NY, :, half:NV], dst_ref=h.at[it, NX, 0:NY, :, half:NV],
                send_sem=edge_send.at[it, NX], recv_sem=edge_recv.at[it, NX],
                device_id=device(-1, 0, me), device_id_type=MESH),
            pltpu.make_async_remote_copy(
                src_ref=h.at[it, NX - 1, 0:NY, :, 0:half], dst_ref=h.at[it, NX, 0:NY, :, 0:half],
                send_sem=edge_send.at[it, NX + 1], recv_sem=edge_recv.at[it, NX + 1],
                device_id=device(1, 0, me), device_id_type=MESH),
        ]

    def send_edges(it, fill):
        def body(at, _):
            x = ordered(at)
            fill(x)
            pack_edge(it, x)
            pl.when(at < PACE[0])(y_copy(it, x).start)
            return 0

        lax.fori_loop(0, 2, body, 0)
        for copy in x_copies(it):
            copy.start()
        lax.fori_loop(2, NX, body, 0)

    def send_more(it, first, last):
        def body(at, _):
            y_copy(it, ordered(at)).start()
            return 0

        lax.fori_loop(first, last, body, 0)

    def stream_cell(it, x, y):
        half = NV // 2
        x_down, x_up = lax.rem(x + NX, NX + 1), x + 1
        y_down, y_up = (y + NY) % (NY + 1), y + 1
        for t in range(6):
            cut = slice(t * 128, (t + 1) * 128)
            own = h[it, x, y, :, cut]
            from_x = h[it, x_down if t < 3 else x_up, y, :, cut]
            if t in (0, 3):
                from_y = h[it, x, y_down, :, cut]
            elif t in (2, 5):
                from_y = h[it, x, y_up, :, cut]
            else:
                from_y = jnp.where(lanes_of(own) < 64, h[it, x, y_down, :, cut], h[it, x, y_up, :, cut])
            up = jnp.broadcast_to(factors[4:5, cut], own.shape) > 0.0
            from_z = jnp.where(up, pltpu.roll(own, 1, 0), pltpu.roll(own, NZ - 1, 0))
            value = (factors[0:1, cut] * own + factors[1:2, cut] * from_x
                     + factors[2:3, cut] * from_y + factors[3:4, cut] * from_z)
            stream[x, y, :, cut] = value * open_cells[x, y * NZ : (y + 1) * NZ, :]

    def stream_inside(it):
        def body(x, _):
            for y in range(1, NY - 1):
                stream_cell(it, x, y)
            return 0

        lax.fori_loop(1, NX - 1, body, 0)

    def stream_ends(it):
        for copy in x_copies(it):
            copy.wait_recv()

        def body(side, _):
            for y in range(1, NY - 1):
                stream_cell(it, side * (NX - 1), y)
            return 0

        lax.fori_loop(0, 2, body, 0)

    def stream_sides(it, first, last):
        def body(at, _):
            x = ordered(at)
            y_copy(it, x).wait_recv()
            stream_cell(it, x, 0)
            stream_cell(it, x, NY - 1)
            if it + 1 < ITERS:
                stream_part[pl.ds(x, 16, stride=NX), :] = projected(stream[x].reshape(CELLS, NV))
            return 0

        lax.fori_loop(first, last, body, 0)

    def rs_copy(it, step):
        target = group(step)
        return pltpu.make_async_remote_copy(
            src_ref=part.at[pl.ds(pl.multiple_of(set_of(target) * 4 * NX, 4 * NX), 4 * NX)], dst_ref=rs.at[it, my_place],
            send_sem=rs_send.at[it, step - 1], recv_sem=rs_recv.at[it, my_place],
            device_id=device(0, 0, target), device_id_type=MESH)

    def rs_wait(it, step):
        at = place_of(step)
        pltpu.make_async_remote_copy(
            src_ref=part.at[0 : 4 * NX], dst_ref=rs.at[it, at],
            send_sem=rs_send.at[it, step - 1], recv_sem=rs_recv.at[it, at],
            device_id=device(0, 0, group(step)), device_id_type=MESH).wait_recv()

    def half_copy(it):
        return pltpu.make_async_remote_copy(
            src_ref=halves.at[it, 0], dst_ref=halves.at[it, 1],
            send_sem=half_send.at[it], recv_sem=half_recv.at[it],
            device_id=device(0, 0, across), device_id_type=MESH)

    def all_copies(it, depth):
        copies = []
        for dy, dx in FAR_FIRST:
            for a, b in mates[::-1] + [(0, 0)]:
                if (a, b, dx, dy) == (0, 0, 0, 0):
                    continue
                slot = dy * 3 + 1 - dx
                cut = rows_read(dx, dy)
                copies.append(pltpu.make_async_remote_copy(
                    src_ref=gathered.at[it, my_set, 1, 0:depth, cut], dst_ref=gathered.at[it, my_set, slot, 0:depth, cut],
                    send_sem=all_send.at[it, len(copies)], recv_sem=all_recv.at[it, my_set, slot],
                    device_id=device(dx, dy, mate(a, b)), device_id_type=MESH))
        return copies

    def for_depth(action):
        for depth in sorted(set(DEPTH)):
            wanted = [at for at in range(SETS) if DEPTH[at] == depth]
            match = my_set == wanted[0]
            for at in wanted[1:]:
                match = jnp.logical_or(match, my_set == at)

            @pl.when(match)
            def _(depth=depth):
                action(depth)

    def wait_all(it):
        for at in range(SETS):
            for slot in range(6):
                dx = 1 - slot % 3
                cut = rows_read(dx, slot // 3)

                def wait(at=at, slot=slot, cut=cut):
                    pltpu.make_async_remote_copy(
                        src_ref=gathered.at[it, at, 1, 0 : DEPTH[at], cut],
                        dst_ref=gathered.at[it, at, slot, 0 : DEPTH[at], cut],
                        send_sem=all_send.at[it, 0], recv_sem=all_recv.at[it, at, slot],
                        device_id=device(0, 0, group(1)), device_id_type=MESH).wait_recv()

                if slot == 1:
                    pl.when(my_set != at)(wait)
                else:
                    wait()

    def tile_copies(it):
        return [
            pltpu.make_async_remote_copy(
                src_ref=tile_row.at[it], dst_ref=tile_mass.at[it, at],
                send_sem=tile_send.at[it, at], recv_sem=tile_recv.at[it, at],
                device_id=device(a, b, me), device_id_type=MESH)
            for at, (a, b) in enumerate(far_tiles)
        ]

    def mass_copies(it):
        return [
            pltpu.make_async_remote_copy(
                src_ref=mass.at[it], dst_ref=mass.at[it],
                send_sem=mass_send.at[it, at], recv_sem=mass_recv.at[it],
                device_id=device(0, 0, mate(a, b)), device_id_type=MESH)
            for at, (a, b) in enumerate(mates)
        ]

    def macro_solve(it):
        def g(c):
            if c == 7:
                return -(g(5) + g(6))
            at, k = SLOTS[c]
            return gathered[it, at, :, k].reshape(ROWS, CELLS)

        def many(*cs):
            return jnp.concatenate([g(c) for c in cs], axis=0)

        flow = many(1, 2, 3, 4)
        along = (many(5, 8, 9, 11), many(8, 6, 10, 12), many(9, 10, 7, 13))
        shifts = ((x_next, x_last), (y_next, y_last), (z_next, z_last))
        total = -6.0 * flow
        for (after, before), a in zip(shifts, along):
            total = total + (after(flow + 0.5 * a) + before(flow - 0.5 * a))
        source[0 : 3 * ROWS] = -0.5 * total[0 : 3 * ROWS]
        source[3 * ROWS :] = -(2.0 / 3.0) * total[3 * ROWS :]
        state[...] = many(0, 1, 2, 3, 4)

        def sweep(_, carry):
            rho, flow = state[0:ROWS], state[ROWS : 5 * ROWS]
            stack = jnp.concatenate([rho + field(flow, 3), flow], axis=0)
            laplace = -6.0 * flow
            grads, divergence = [], None
            for d, (after, before) in enumerate(shifts):
                up, down = after(stack), before(stack)
                laplace = laplace + (up[ROWS:] + down[ROWS:])
                grads.append(0.5 * (field(up, 0) - field(down, 0)))
                part_div = 0.5 * (field(up, 1 + d) - field(down, 1 + d))
                divergence = part_div if divergence is None else divergence + part_div
            state[0:ROWS] = rho - STEP * divergence
            for d in range(3):
                state[(1 + d) * ROWS : (2 + d) * ROWS] = field(flow, d) + STEP * (
                    -0.5 * grads[d] + 0.5 * field(laplace, d) + source[d * ROWS : (d + 1) * ROWS])
            state[4 * ROWS :] = field(flow, 3) + STEP * (
                -(2.0 / 3.0) * divergence + (2.0 / 3.0) * field(laplace, 3) + source[3 * ROWS :])
            return carry

        lax.fori_loop(0, MACRO_STEPS, sweep, 0)

    def coefficients(it):
        shift = target_ref[0, 0] - jnp.sum(mass[it]) / float(NX * NY * NZ * n_tx * n_ty)
        state[0:ROWS] = state[0:ROWS] + shift
        now = state[...]
        was = jnp.concatenate([gathered[it, SLOTS[c][0], :, SLOTS[c][1]].reshape(ROWS, CELLS) for c in range(5)], axis=0)
        change = now - was
        fluid = wall_rows[0]

        def tile(value, half):
            return value.reshape(5, 2, ROWS // 2, CELLS)[:, half, NX : 2 * NX].reshape(5 * NX, CELLS)

        def along_x(value):
            return value.reshape(5, ROWS // 2, CELLS)[:, NX : 2 * NX].reshape(5 * NX, CELLS)

        def put(at, value):
            coef[at * 5 * NX : (at + 1) * 5 * NX, :] = (value.reshape(5, NX, CELLS) * fluid[None]).reshape(5 * NX, CELLS)

        here, other = tile(change, 0), tile(change, 1)
        strip = change.reshape(5, 2, ROWS // 2, CELLS)[:, 0].reshape(5 * ROWS // 2, CELLS)
        lane = lanes_of(here)
        put(0, 0.9 * here + STEP * tile(now, 0))
        put(1, along_x(x_last(strip)) - here)
        put(2, along_x(x_next(strip)) - here)
        put(3, jnp.where(lane >= NZ, pltpu.roll(here, NZ, 1), pltpu.roll(other, NZ, 1)) - here)
        put(4, jnp.where(lane < CELLS - NZ, pltpu.roll(here, CELLS - NZ, 1), pltpu.roll(other, CELLS - NZ, 1)) - here)
        put(5, z_last(here) - here)
        put(6, z_next(here) - here)
        for x in range(NX):
            c = coef[pl.ds(x, COEF, stride=NX), :]
            c_high = rounded(c)
            coef3[x] = jnp.concatenate([c_high, c - c_high, c_high, jnp.zeros((8, CELLS), f32)], axis=0).astype(bf16)

    def place(it, x, value):
        part[pl.ds(x, 16, stride=NX), :] = value

    for it in range(ITERS):
        if it == 0:
            for x in range(NX):
                loads[x].wait()
                place(0, x, projected(plane(0, x)))
            greeted = ring + 4 * len(near_tiles)

            @pl.when(my_set == MASS)
            def _():
                pl.semaphore_wait(barrier, greeted + len(only_far))

            @pl.when(my_set != MASS)
            def _():
                pl.semaphore_wait(barrier, greeted)

        for step in sorted(range(1, ring), key=lambda at: abs(at - ring // 2)):
            rs_copy(it, step).start()

        def finalize(x, it=it):
            if it > 0:
                new = stream[x].reshape(CELLS, NV) + tn(coef3[x], rows3[...])
                h[it, x, 0:NY] = new.reshape(NY, NZ, NV)

        send_edges(it, finalize)
        if it == 0:
            prepare()

        rs[it, my_place] = part[pl.ds(pl.multiple_of(my_set * 4 * NX, 4 * NX), 4 * NX), :]
        for step in range(1, ring):
            rs_wait(it, step)
        total = rs[it, 0]
        for at in range(1, ring):
            total = total + rs[it, at]
        halves[it, 0] = total
        half_copy(it).start()
        send_more(it, PACE[0], PACE[1])
        stream_inside(it)
        half_copy(it).wait_recv()
        gathered[it, my_set, 1] = (total + halves[it, 1]).reshape(4, NX, CELLS)

        def send_all(depth, it=it):
            for copy in all_copies(it, depth):
                copy.start()

        for_depth(send_all)

        @pl.when(my_set == MASS)
        def _(it=it):
            tile_row[it] = jnp.sum(gathered[it, my_set, 1, 3], axis=0, keepdims=True)
            for copy in tile_copies(it):
                copy.start()

        send_more(it, PACE[1], NX)

        if it == 0:
            prepare_rows()
        stream_ends(it)
        stream_sides(it, 0, EARLY)

        @pl.when(my_set == MASS)
        def _(it=it):
            total = tile_row[it]
            for at, copy in enumerate(tile_copies(it)):
                copy.wait_recv()
                total = total + tile_mass[it, at]
            mass[it] = total
            for copy in mass_copies(it):
                copy.start()

        wait_all(it)
        macro_solve(it)
        stream_sides(it, EARLY, NX)

        @pl.when(my_set != MASS)
        def _(it=it):
            mass_copies(it)[0].wait_recv()

        coefficients(it)

        for step in range(1, ring):
            rs_copy(it, step).wait_send()
        if it + 1 < ITERS:
            for x in range(NX):
                at = pl.ds(x, 16, stride=NX)
                part[at, :] = stream_part[at, :] + jnp.dot(mixed3[...], coef3[x], preferred_element_type=f32)

    for x in range(NX):
        new = stream[x].reshape(CELLS, NV) + tn(coef3[x], rows3[...])
        dist_ref[x] = new.reshape(NY, NZ, NV)
    for k in range(5):
        value = state[k * ROWS + NX : k * ROWS + 2 * NX, :]
        for y in range(NY):
            moved = value if y == 0 else pltpu.roll(value, CELLS - y * NZ, 1)
            macro_ref[k, :, y, :] = moved[:, 0:NZ]

    for it in range(ITERS):
        half_copy(it).wait_send()
        for copy in x_copies(it):
            copy.wait_send()

        def sent(x, _, it=it):
            y_copy(it, x).wait_send()
            return 0

        lax.fori_loop(0, NX, sent, 0)

        def sent_all(depth, it=it):
            for copy in all_copies(it, depth):
                copy.wait_send()

        for_depth(sent_all)

        @pl.when(my_set == MASS)
        def _(it=it):
            for copy in tile_copies(it):
                copy.wait_send()
            for copy in mass_copies(it):
                copy.wait_send()


def on_device(sizes, initial, velocity, weights, wall, wall_temp, mass_target):
    n_tx, n_ty, n_vel = sizes
    dma = pltpu.SemaphoreType.DMA
    vmem = pl.BlockSpec(memory_space=pltpu.VMEM)
    tiles = n_tx * n_ty - 1
    return pl.pallas_call(
        functools.partial(kernel, sizes),
        out_shape=(jax.ShapeDtypeStruct((NX, NY, NZ, NV), f32), jax.ShapeDtypeStruct((5, NX, NY, NZ), f32)),
        in_specs=[pl.BlockSpec(memory_space=pltpu.HBM)] * 5 + [pl.BlockSpec(memory_space=pltpu.SMEM)],
        out_specs=(vmem, vmem),
        scratch_shapes=[
            pltpu.VMEM((ITERS, NX + 1, NY + 1, NZ, NV), f32),
            pltpu.VMEM((NX, NY, NZ, NV), f32),
            pltpu.VMEM((ITERS, NX, NZ, NV), f32),
            pltpu.VMEM((16 * NX, CELLS), f32),
            pltpu.VMEM((16 * NX, CELLS), f32),
            pltpu.VMEM((ITERS, n_vel // 2, 4 * NX, CELLS), f32),
            pltpu.VMEM((ITERS, 2, 4 * NX, CELLS), f32),
            pltpu.VMEM((ITERS, SETS, 6, 4, NX, CELLS), f32),
            pltpu.VMEM((ITERS, 1, CELLS), f32),
            pltpu.VMEM((ITERS, tiles, 1, CELLS), f32),
            pltpu.VMEM((ITERS, 1, CELLS), f32),
            pltpu.VMEM((COEF * NX, CELLS), f32),
            pltpu.VMEM((NX, 128, CELLS), bf16),
            pltpu.VMEM((128, NV), f32),
            pltpu.VMEM((128, NV), bf16),
            pltpu.VMEM((16, NV), f32),
            pltpu.VMEM((32, NV), bf16),
            pltpu.VMEM((16, 128), bf16),
            pltpu.VMEM((8, NV), f32),
            pltpu.VMEM((NX, CELLS, 128), f32),
            pltpu.VMEM((1, NX, CELLS), f32),
            pltpu.VMEM((5 * ROWS, CELLS), f32),
            pltpu.VMEM((4 * ROWS, CELLS), f32),
            pltpu.VMEM((3, NV), f32), pltpu.VMEM((NV,), f32),
            pltpu.VMEM((NX, NY, NZ), jnp.int32), pltpu.VMEM((NX, NY, NZ), f32),
            dma((NX,)), dma((4,)),
            dma((ITERS, n_vel // 2 - 1)), dma((ITERS, n_vel // 2)),
            dma((ITERS,)), dma((ITERS,)),
            dma((ITERS, 23)), dma((ITERS, SETS, 6)),
            dma((ITERS, tiles)), dma((ITERS, tiles)),
            dma((ITERS, 3)), dma((ITERS,)),
            dma((ITERS, NX + 2)), dma((ITERS, NX + 2)),
        ],
        compiler_params=pltpu.CompilerParams(collective_id=0, has_side_effects=True, vmem_limit_bytes=48 * 1024 * 1024),
    )(
        initial,
        *(pltpu.with_memory_space_constraint(a, pltpu.HBM) for a in (velocity, weights, wall, wall_temp)),
        mass_target.reshape(1, 1),
    )


def solution(mesh):
    sizes = (mesh.shape["tx"], mesh.shape["ty"], mesh.shape["vel"])
    placed = (
        P("tx", "ty", None, "vel"),
        P(None, "vel"),
        P("vel"),
        P("tx", "ty", None),
        P("tx", "ty", None),
        P(),
    )
    return jax.shard_map(
        functools.partial(on_device, sizes),
        mesh=mesh,
        in_specs=placed,
        out_specs=(P("tx", "ty", None, "vel"), P(None, "tx", "ty", None)),
        check_vma=False,
    )
```
